256 devices in a mesh: ctx: 32 (over y, z), tp: 8 (over x, core).
Axes of the slice: x: 4, y: 4, z: 8, core: 2. Of those that a mesh axis runs over, the one named last changes fastest.
Arguments:
- q_in: bfloat16 [8192, 8192], P('ctx', 'tp'), may hold values from -10.5 to 10.5
- k_in: bfloat16 [8192, 8192], P('ctx', 'tp'), may hold values from -6 to 6
- v_in: bfloat16 [8192, 8192], P('ctx', 'tp'), may hold values from -6 to 6
- grad_out: bfloat16 [8192, 8192], P('ctx', 'tp'), may hold values from -6 to 6
- doc_ids: int32 [8192], P('ctx'), may hold values from 0 to 3, never falling along the last dimension, each value on 1 to 4096 neighbouring positions
- gain: bfloat16 [8192], P('tp'), may hold values from 0.099609375 to 1.8984375
- filters: bfloat16 [512, 128], P('tp'), may hold values from -0.5 to 0.5
- short_weight: bfloat16 [3, 3, 8192], P(None, None, 'tp'), may hold values from -3.5 to 3.5
Outputs:
- grad_q: bfloat16 [8192, 8192], P('ctx', 'tp')
- grad_k: bfloat16 [8192, 8192], P('ctx', 'tp')
- grad_v: bfloat16 [8192, 8192], P('ctx', 'tp')
- grad_gain: float32 [8192], P('tp')
- grad_filters: float32 [512, 128], P('tp')
- grad_short: float32 [3, 3, 8192], P(None, None, 'tp')
The draws below stay inside these ranges and needn't reach their ends.
Inputs may be any that keep to these rules, and one draw needn't show every extreme that they name: doc_ids never fall along the window, so every document is one run of consecutive tokens; one document covers exactly 4096 tokens.
All inputs are finite; a program needn't handle non-finite values.
Results may differ from the reference program's by a relative error of at most 0.0049.
Values may be sent and summed in bfloat16 or wider, within the bound.
A program may use at most 128 MiB of HBM per device.

```python
import math
import jax
import jax.numpy as jnp
import numpy as np
from jax import lax

D = 8192
GROUP = 16
TAPS = 128
SHORT = 3
FILTERS = 512
TOKENS = 8192
DOCS = 4
DOC_MOST = 4096


def draw_q_in(key, part):
    position = jnp.arange(D, dtype=jnp.float32) / D
    base = jnp.clip(jax.random.normal(key, (TOKENS, D), jnp.float32), -6.0, 6.0)
    col_scale = 1.0 + 0.75 * position
    return (base * col_scale[None, :]).astype(jnp.bfloat16)


def block_scale(rng, shape, pieces, smallest, top_value):
    level, own = 1.0, jax.random.fold_in(rng, 6)
    for dim, parts in pieces:
        heights = jnp.exp(jax.random.uniform(jax.random.fold_in(own, dim), (parts,), jnp.float32, smallest / len(pieces), top_value / len(pieces)))
        level = level * jnp.repeat(heights, shape[dim] // parts).reshape([-1 if axis == dim else 1 for axis in range(len(shape))])
    return level


def split_up(number_of, total, limit, skew):
    portions = [(1 << 20) // math.isqrt(standing ** skew) + 1 for standing in range(2, number_of + 1)]
    rest, counts = total - limit - (number_of - 1), [1] * (number_of - 1)
    while rest > 0:
        free = [i for i in range(number_of - 1) if counts[i] < limit]
        pool, budget = sum([portions[i] for i in free]), rest
        for i in free:
            addition = min(limit - counts[i], max(1, budget * portions[i] // pool), rest)
            counts[i] = counts[i] + addition
            rest = rest - addition
    return np.array([limit] + counts)


def ragged_sizes(stream_key, count, total, reach, lean):
    if count == 2:
        one = jax.random.randint(stream_key, (), max(1, total - reach), min(reach, total - 1) + 1)
        return jnp.stack([one, total - one])
    tallies = jnp.asarray(split_up(count, total, reach, lean), jnp.int32)
    twos = (count - 1) // 2
    giver, taker = tallies[1:1 + 2 * twos:2], tallies[2:2 + 2 * twos:2]
    margin = jnp.minimum(giver - 1, reach - taker)
    shifted = jax.random.randint(jax.random.fold_in(stream_key, 1), (twos,), 0, 1 << 20) % (margin + 1)
    tallies = tallies.at[1:1 + 2 * twos:2].set(giver - shifted).at[2:2 + 2 * twos:2].set(taker + shifted)
    return tallies[jax.random.permutation(jax.random.fold_in(stream_key, 2), count)]


def centred(key, dims, width, bound, shards=(), held_as=jnp.bfloat16):
    loudness = block_scale(key, dims, shards, -0.22, 0.18) if shards else 1.0
    result = jax.random.normal(key, dims, jnp.float32) * width * loudness
    return jnp.minimum(jnp.maximum(result, -bound), bound).astype(held_as)


def setup_inputs(seed: int = 0) -> dict:
    splits = jax.random.split(jax.random.key(seed), 9)
    q_in = draw_q_in(jax.random.fold_in(splits[8], 71), 0)
    k_in = centred(splits[1], (TOKENS, D), 1.0, 6.0, ((0, 32), (1, 8)))
    v_in = centred(splits[2], (TOKENS, D), 1.0, 6.0, ((0, 32), (1, 8)))
    grad_out = centred(splits[3], (TOKENS, D), 1.0, 6.0, ((0, 32), (1, 8)))
    doc_ids = jnp.searchsorted(jnp.cumsum(ragged_sizes(splits[4], DOCS, TOKENS, DOC_MOST, 2)), jnp.arange(TOKENS), side="right").astype(jnp.int32)
    gain = jnp.clip(1.0 + 0.18 * jax.random.normal(splits[5], (D,), jnp.float32), 0.099609375, 1.8984375).astype(jnp.bfloat16)
    filters = centred(splits[6], (FILTERS, TAPS), TAPS ** -0.5, 0.5, ((0, 8),))
    short_weight = centred(splits[7], (3, SHORT, D), SHORT ** -0.5, 3.5, ((2, 8),))
    return dict(q_in=q_in, k_in=k_in, v_in=v_in, grad_out=grad_out, doc_ids=doc_ids, gain=gain, filters=filters, short_weight=short_weight)


def before(values, offset, fill):
    padding = jnp.full((TAPS,) + values.shape[1:], fill, values.dtype)
    joined = jnp.concatenate([padding, values], axis=0)
    return lax.dynamic_slice_in_dim(joined, TAPS - offset, values.shape[0], 0)

def ahead_of(values, offset, fill):
    padding = jnp.full((TAPS,) + values.shape[1:], fill, values.dtype)
    joined = jnp.concatenate([values, padding], axis=0)
    return lax.dynamic_slice_in_dim(joined, offset, values.shape[0], 0)

def feature(inputs, weights, doc_ids):
    input_f = inputs.astype(jnp.float32)
    weight_f = weights.astype(jnp.float32)
    running = jnp.zeros(input_f.shape, jnp.float32)
    for offset in range(SHORT):
        agree = (before(doc_ids, offset, -1) == doc_ids).astype(jnp.float32)[:, None]
        running = running + weight_f[offset][None, :] * before(input_f, offset, 0.0) * agree
    return running

def reference(q_in, k_in, v_in, grad_out, doc_ids, gain, filters, short_weight):
    block_cols = min(D, 1024)
    block_count = D // block_cols
    filter_block = block_cols // GROUP
    grad_scale = 1.0 / math.sqrt(TOKENS)

    def columns(values, index, axis):
        return lax.dynamic_slice_in_dim(values, (index * block_cols).astype(jnp.int32), block_cols, axis)

    def forward_block(index):
        q_cols = columns(q_in, index, 1)
        k_cols = columns(k_in, index, 1)
        v_cols = columns(v_in, index, 1)
        weight_cols = columns(short_weight, index, 2)
        filter_rows = lax.dynamic_slice_in_dim(filters, (index * filter_block).astype(jnp.int32), filter_block, 0)
        feat_q = feature(q_cols, weight_cols[0], doc_ids)
        feat_k = feature(k_cols, weight_cols[1], doc_ids)
        feat_v = feature(v_cols, weight_cols[2], doc_ids)
        product = (feat_k * feat_v).astype(jnp.bfloat16)
        product_f = lax.optimization_barrier(product).astype(jnp.float32)
        tap_table = jnp.repeat(filter_rows.astype(jnp.float32), GROUP, axis=0)

        def add_tap(offset, running):
            offset = offset.astype(jnp.int32)
            coeff = lax.dynamic_index_in_dim(tap_table, offset, 1, keepdims=False)
            agree = (before(doc_ids, offset, -1) == doc_ids).astype(jnp.float32)[:, None]
            return running + coeff[None, :] * before(product_f, offset, 0.0) * agree
        mixed = lax.fori_loop(0, TAPS, add_tap, jnp.zeros(product_f.shape, jnp.float32))
        return (q_cols, k_cols, v_cols, weight_cols, tap_table, feat_q, feat_k, feat_v, product_f, mixed, feat_q * mixed)

    def gather_stats(index, carry):
        square_sum, inner_sum = carry
        index = index.astype(jnp.int32)
        y_out = forward_block(index)[-1]
        weighted = columns(gain, index, 0).astype(jnp.float32)[None, :] * columns(grad_out, index, 1).astype(jnp.float32)
        return (square_sum + lax.optimization_barrier(jnp.sum(y_out * y_out, axis=1)), inner_sum + lax.optimization_barrier(jnp.sum(weighted * y_out, axis=1)))
    zero_rows = jnp.zeros((TOKENS,), jnp.float32)
    square_sum, inner_sum = lax.fori_loop(0, block_count, gather_stats, (zero_rows, zero_rows))
    row_scale = lax.rsqrt(square_sum / D + 1e-06)

    def backward_block(index):
        q_cols, k_cols, v_cols, weight_cols, tap_table, feat_q, feat_k, feat_v, product_f, mixed, y_out = forward_block(index)
        cot_out = columns(grad_out, index, 1).astype(jnp.float32)
        gain_cols = columns(gain, index, 0).astype(jnp.float32)
        weighted = gain_cols[None, :] * cot_out
        grad_y = row_scale[:, None] * weighted - y_out * (row_scale ** 3 * inner_sum / D)[:, None]
        grad_gain = lax.optimization_barrier(jnp.sum(cot_out * y_out * row_scale[:, None], axis=0)) * grad_scale
        grad_fq = grad_y * mixed
        grad_mixed16 = (grad_y * feat_q).astype(jnp.bfloat16)
        grad_mixed = lax.optimization_barrier(grad_mixed16).astype(jnp.float32)

        def add_tap(offset, carry):
            running, filter_rows = carry
            offset = offset.astype(jnp.int32)
            coeff = lax.dynamic_index_in_dim(tap_table, offset, 1, keepdims=False)
            ahead = (ahead_of(doc_ids, offset, -1) == doc_ids).astype(jnp.float32)[:, None]
            running = running + coeff[None, :] * ahead_of(grad_mixed, offset, 0.0) * ahead
            behind = (before(doc_ids, offset, -1) == doc_ids).astype(jnp.float32)[:, None]
            tap_term = lax.optimization_barrier(jnp.sum(grad_mixed * before(product_f, offset, 0.0) * behind, axis=0))
            tap_term = tap_term.reshape(filter_block, GROUP).sum(axis=1)
            filter_rows = lax.dynamic_update_index_in_dim(filter_rows, tap_term, offset, 0)
            return (running, filter_rows)
        grad_prod, filter_rows = lax.fori_loop(0, TAPS, add_tap, (jnp.zeros(grad_mixed.shape, jnp.float32), jnp.zeros((TAPS, filter_block), jnp.float32)))
        grad_fk = grad_prod * feat_v
        grad_fv = grad_prod * feat_k
        input_grads = []
        short_grads = []
        for branch, (inputs, grad_feat) in enumerate(((q_cols, grad_fq), (k_cols, grad_fk), (v_cols, grad_fv))):
            weight_f = weight_cols[branch].astype(jnp.float32)
            input_f = inputs.astype(jnp.float32)
            running = jnp.zeros(grad_feat.shape, jnp.float32)
            tap_rows = []
            for offset in range(SHORT):
                ahead = (ahead_of(doc_ids, offset, -1) == doc_ids).astype(jnp.float32)[:, None]
                running = running + weight_f[offset][None, :] * ahead_of(grad_feat, offset, 0.0) * ahead
                behind = (before(doc_ids, offset, -1) == doc_ids).astype(jnp.float32)[:, None]
                tap_rows.append(lax.optimization_barrier(jnp.sum(grad_feat * before(input_f, offset, 0.0) * behind, axis=0)))
            input_grads.append(running.astype(jnp.bfloat16))
            short_grads.append(jnp.stack(tap_rows) * grad_scale)
        return (input_grads[0], input_grads[1], input_grads[2], grad_gain, filter_rows.T * grad_scale, jnp.stack(short_grads))
    results = lax.map(backward_block, jnp.arange(block_count, dtype=jnp.int32))

    def merge_cols(values):
        return jnp.transpose(values, (1, 0, 2)).reshape(TOKENS, D)
    grad_q = merge_cols(results[0])
    grad_k = merge_cols(results[1])
    grad_v = merge_cols(results[2])
    grad_gain = results[3].reshape(D)
    grad_filters = results[4].reshape(D // GROUP, TAPS)
    grad_short = jnp.transpose(results[5], (1, 2, 0, 3)).reshape(3, SHORT, D)
    return (grad_q, grad_k, grad_v, grad_gain, grad_filters, grad_short)
```

```python
import functools
import math

import jax
import jax.numpy as jnp
from jax import lax
from jax.experimental import pallas as pl
from jax.experimental.pallas import tpu as pltpu
from jax.sharding import PartitionSpec as P

F32 = jnp.float32
BF16 = jnp.bfloat16
MESH = pl.DeviceIdType.MESH
LANES = 128
HALF = 128
ROWS = 256
SHORT = 3
EPS = 1e-06
RING = 8
CHUNK = 24


def iota(axis):
    return lax.broadcasted_iota(jnp.int32, (LANES, LANES), axis)


def as_column(row, flipped=False):
    eye = flip() if flipped else iota(0) == iota(1)
    spread = jnp.where(eye, jnp.broadcast_to(row, (LANES, LANES)), 0.0)
    return jnp.sum(spread, axis=1, keepdims=True)


def flip():
    return iota(0) + iota(1) == LANES - 1


def mirror():
    total = iota(0) + iota(1)
    return jnp.where((total == 0) | (total == LANES), 1.0, 0.0)


def kernel(
    ny,
    nz,
    ntp,
    q_hbm,
    k_hbm,
    v_hbm,
    go_hbm,
    docs_ref,
    gain_ref,
    filt_ref,
    sw_ref,
    gq_hbm,
    gk_hbm,
    gv_hbm,
    gain_out,
    filt_out,
    short_out,
    xin,
    go_v,
    xf,
    feats,
    mixed,
    y_s,
    grads,
    outs,
    prod,
    gmix,
    tf,
    tb,
    fmask,
    bmask,
    fmask32,
    filt32,
    filt_rev,
    wsc,
    dcol,
    m1,
    m2,
    docs_prev,
    docs_next,
    edge_s,
    edge_r,
    tail_s,
    tail_r,
    acc,
    stats,
    scales,
    big,
    small,
    lhs_s,
    red,
    red_a,
    red_b,
    fin,
    load_sem,
    store_sem,
    doc_sem,
    edge_sem,
    h1_send,
    h1_recv,
    h2_send,
    h2_recv,
    st_send,
    st_recv,
    ra_send,
    ra_recv,
    rb_send,
    rb_recv,
    rc_send,
    rc_recv,
):
    nt = nz
    groups = filt_ref.shape[0]
    per_tile = groups // nt
    width = LANES // per_tile
    n_ctx = ny * nz
    channels = nt * LANES
    total_channels = channels * ntp
    grad_scale = 1.0 / math.sqrt(ROWS * n_ctx)
    ctx = lax.axis_index("ctx")
    tp = lax.axis_index("tp")
    nxt = lax.rem(ctx + 1, n_ctx)
    prv = lax.rem(ctx + n_ctx - 1, n_ctx)
    y_at = lax.div(ctx, nz)
    z_at = lax.rem(ctx, nz)

    def z_peer(d):
        return lax.rem(z_at + d, nz)

    def y_peer(d):
        return lax.rem(y_at + d, ny)

    def tp_peer(d):
        return lax.rem(tp + d, ntp)

    def remote(src, dst, send, recv, where):
        return pltpu.make_async_remote_copy(
            src_ref=src, dst_ref=dst, send_sem=send, recv_sem=recv, device_id=where, device_id_type=MESH
        )

    loads = [
        pltpu.make_async_copy(k_hbm, xin.at[1], load_sem.at[1]),
        pltpu.make_async_copy(v_hbm, xin.at[2], load_sem.at[2]),
        pltpu.make_async_copy(q_hbm, xin.at[0], load_sem.at[0]),
        pltpu.make_async_copy(go_hbm, go_v, load_sem.at[3]),
    ]
    for load in loads:
        load.start()

    barrier = pltpu.get_barrier_semaphore()
    partners = [(nxt, tp), (prv, tp)]
    partners += [(ctx, tp_peer(d)) for d in range(1, ntp)]
    partners += [(y_at * nz + z_peer(d), tp) for d in range(1, nz)]
    partners += [(y_peer(d) * nz + z_at, tp) for d in range(1, ny)]
    for where in partners:
        pl.semaphore_signal(barrier, inc=1, device_id=where, device_id_type=MESH)

    for a in range(3):
        taps = sw_ref[a].astype(F32)
        for c in range(nt):
            wsc[c, a, 0:SHORT, :] = taps[:, c * LANES : (c + 1) * LANES]
    gain_row = gain_ref[...].astype(F32)
    for c in range(nt):
        wsc[c, 3, 0:1, :] = gain_row[:, c * LANES : (c + 1) * LANES]
    filt32[...] = filt_ref[...].astype(F32)
    filt_rev[...] = jnp.dot(filt_ref[...], mirror().astype(BF16), preferred_element_type=F32)

    docs_f = docs_ref[...].astype(F32)
    own = [docs_f[0:1], docs_f[1:2]]
    own_col = [as_column(row) for row in own]
    for n in range(2):
        dcol[8 + HALF * n : 8 + HALF * (n + 1), :] = jnp.broadcast_to(own_col[n], (HALF, LANES))

    def short_masks(start, size):
        here = dcol[8 + start : 8 + start + size, :]
        m1[start : start + size, :] = (dcol[7 + start : 7 + start + size, :] == here).astype(F32)
        m2[start : start + size, :] = (dcol[6 + start : 6 + start + size, :] == here).astype(F32)

    short_masks(HALF, HALF)

    for load in loads[:3]:
        load.wait()
    for a in range(3):
        last = xin[a, ROWS - 16 : ROWS, :].astype(F32)
        edge_s[2 * a : 2 * a + 2, :] = last[14:16]
    edge_s[6:8, :] = jnp.zeros((2, channels), F32)

    pl.semaphore_wait(barrier, len(partners))

    doc_fwd = remote(docs_ref, docs_prev, doc_sem.at[0], doc_sem.at[1], (nxt, tp))
    doc_bwd = remote(docs_ref, docs_next, doc_sem.at[2], doc_sem.at[3], (prv, tp))
    edge = remote(edge_s, edge_r, edge_sem.at[0], edge_sem.at[1], (nxt, tp))
    doc_fwd.start()
    doc_bwd.start()
    edge.start()

    def cols(c):
        return pl.ds(pl.multiple_of(c * LANES, LANES), LANES)

    def feature(a, c, start):
        x0 = xf[a, c, pl.ds(8 + start, HALF), :]
        x1 = xf[a, c, pl.ds(7 + start, HALF), :]
        x2 = xf[a, c, pl.ds(6 + start, HALF), :]
        w = wsc[c, a]
        return (
            w[0:1] * x0
            + w[1:2] * x1 * m1[start : start + HALF, :]
            + w[2:3] * x2 * m2[start : start + HALF, :]
        )

    def halo1(c):
        return remote(
            prod.at[c, pl.ds(ROWS, HALF)], prod.at[c, pl.ds(0, HALF)], h1_send.at[c], h1_recv.at[c], (nxt, tp)
        )

    def halo2(c):
        return remote(
            gmix.at[c, pl.ds(0, HALF)], gmix.at[c, pl.ds(ROWS, HALF)], h2_send.at[c], h2_recv.at[c], (prv, tp)
        )

    def products(c, start):
        fk = feature(1, c, start)
        fv = feature(2, c, start)
        feats[1, c, start : start + HALF, :] = fk
        feats[2, c, start : start + HALF, :] = fv
        prod[c, HALF + start : 2 * HALF + start, :] = (fk * fv).astype(BF16)

    def late_half(c, carry):
        for a in (1, 2):
            xf[a, c, 8 : 8 + ROWS, :] = xin[a, :, cols(c)].astype(F32)
        products(c, HALF)
        halo1(c).start()
        return carry

    lax.fori_loop(0, nt, late_half, 0)

    doc_fwd.wait_recv()
    doc_bwd.wait_recv()
    edge.wait_recv()
    row_prev = jnp.where(ctx == 0, -1.0, docs_prev[1:2, :].astype(F32))
    row_next = jnp.where(ctx == n_ctx - 1, -1.0, docs_next[0:1, :].astype(F32))
    col_prev = as_column(row_prev)
    col_next = as_column(row_next)
    dcol[0:8, :] = jnp.broadcast_to(col_prev[HALF - 8 :], (8, LANES))
    dcol[8 + ROWS : 16 + ROWS, :] = jnp.broadcast_to(col_next[:8], (8, LANES))
    short_masks(0, HALF)
    short_masks(ROWS, 8)
    i_at, j_at = iota(0), iota(1)

    def pick(keep, column, row):
        return jnp.where(keep & (column == row), 1.0, 0.0)

    i_back = LANES - 1 - i_at
    back_col = [as_column(row, True) for row in own]
    before_rows = (row_prev, own[0])
    after_rows = (own[1], row_next)
    for n in range(2):
        fmask[n, :, 0:LANES] = pick(j_at > i_at, own_col[n], before_rows[n]).astype(BF16)
        fmask[n, :, LANES:] = pick(j_at <= i_at, own_col[n], own[n]).astype(BF16)
        fmask32[n, :, 0:LANES] = pick(j_at > i_back, back_col[n], before_rows[n])
        fmask32[n, :, LANES:] = pick(j_at <= i_back, back_col[n], own[n])
        bmask[n, :, 0:LANES] = pick(j_at >= i_at, own_col[n], own[n]).astype(BF16)
        bmask[n, :, LANES:] = pick(j_at < i_at, own_col[n], after_rows[n]).astype(BF16)

    def build(source, masks, target):
        def one(g, carry):
            c, at = lax.div(g, per_tile), lax.rem(g, per_tile)
            row = jnp.broadcast_to(source[pl.ds(g, 1), :], (HALF, LANES))
            band = pltpu.roll(row, 0, 1, stride=1, stride_axis=0).astype(BF16)
            rows = pl.ds(pl.multiple_of(at * HALF, HALF), HALF)
            for n in range(2):
                target[n, c, rows, 0:LANES] = band * masks[n, :, 0:LANES]
                target[n, c, rows, LANES:] = band * masks[n, :, LANES:]
            return carry

        lax.fori_loop(0, groups, one, 0)

    build(filt_rev, fmask, tf)

    def early_half(c, carry):
        xf[0, c, 8 : 8 + ROWS, :] = xin[0, :, cols(c)].astype(F32)
        for a in range(3):
            xf[a, c, 6:8, :] = edge_r[2 * a : 2 * a + 2, cols(c)]
        products(c, 0)
        for start in (0, HALF):
            feats[0, c, start : start + HALF, :] = feature(0, c, start)
        return carry

    lax.fori_loop(0, nt, early_half, 0)
    loads[3].wait()

    lane_group = lax.div(iota(1), width)

    def convolve(bands, window):
        small[...] = jnp.dot(bands, window, preferred_element_type=F32)
        value = small[0:HALF, :]
        for g in range(1, per_tile):
            value = jnp.where(lane_group == g, small[g * HALF : (g + 1) * HALF, :], value)
        return value

    acc[...] = jnp.zeros_like(acc)

    def forward(n):
        span = slice(n * HALF, (n + 1) * HALF)

        def one(c, carry):
            if n == 0:
                halo1(c).wait_recv()
            value = convolve(tf[n, c], prod[c, n * HALF : n * HALF + ROWS, :])
            mixed[c, span, :] = value
            y = feats[0, c, span, :] * value
            y_s[c, span, :] = y
            weighted = wsc[c, 3, 0:1, :] * go_v[span, cols(c)].astype(F32)
            acc[n, 0] += y * y
            acc[n, 1] += weighted * y
            return carry

        lax.fori_loop(0, nt, one, 0)

    forward(1)
    forward(0)

    stats[tp] = jnp.zeros((8, LANES), F32)
    for n in range(2):
        for kind in range(2):
            line = jnp.sum(acc[n, kind].T, axis=0, keepdims=True)
            stats[tp, 2 * kind + n : 2 * kind + n + 1, :] = line
    sends = [
        remote(stats.at[tp], stats.at[tp], st_send.at[d], st_recv.at[d], (ctx, tp_peer(d)))
        for d in range(1, ntp)
    ]
    for send in sends:
        send.start()
    build(filt32, bmask, tb)
    for d in range(1, ntp):
        came = stats.at[tp_peer(ntp - d)]
        remote(came, came, st_send.at[d], st_recv.at[d], (ctx, tp_peer(d))).wait_recv()
    sums = stats[0]
    for p in range(1, ntp):
        sums = sums + stats[p]
    scale = lax.rsqrt(sums[0:2] / total_channels + EPS)
    pull = scale * scale * scale * sums[2:4] / total_channels
    for n in range(2):
        scales[n, 0] = jnp.broadcast_to(as_column(scale[n : n + 1]), (HALF, LANES))
        scales[n, 1] = jnp.broadcast_to(as_column(pull[n : n + 1]), (HALF, LANES))

    def backward_norm(n):
        span = slice(n * HALF, (n + 1) * HALF)

        def one(c, carry):
            cot = go_v[span, cols(c)].astype(F32)
            y = y_s[c, span, :]
            row_scale = scales[n, 0]
            grad_y = row_scale * (wsc[c, 3, 0:1, :] * cot) - y * scales[n, 1]
            gain_part = jnp.sum(cot * y * row_scale, axis=0, keepdims=True)
            if n == 0:
                red[c, 17:18, :] = gain_part
            else:
                red[c, 17:18, :] += gain_part
            gmix[c, span, :] = (grad_y * feats[0, c, span, :]).astype(BF16)
            if n == 0:
                halo2(c).start()
            grads[0, c, span, :] = grad_y * mixed[c, span, :]
            if n == 0:
                tail_s[0:2, cols(c)] = grads[0, c, 0:2, :]
            return carry

        lax.fori_loop(0, nt, one, 0)

    backward_norm(0)
    backward_norm(1)

    def backward_conv(n):
        span = slice(n * HALF, (n + 1) * HALF)

        def one(c, carry):
            if n == 1:
                halo2(c).wait_recv()
            value = convolve(tb[n, c], gmix[c, n * HALF : n * HALF + ROWS, :])
            grads[1, c, span, :] = value * feats[2, c, span, :]
            grads[2, c, span, :] = value * feats[1, c, span, :]
            if n == 0:
                tail_s[2:4, cols(c)] = grads[1, c, 0:2, :]
                tail_s[4:6, cols(c)] = grads[2, c, 0:2, :]
            return carry

        lax.fori_loop(0, nt, one, 0)

    tail_s[6:8, :] = jnp.zeros((2, channels), F32)
    backward_conv(0)
    tail = remote(tail_s, tail_r, edge_sem.at[2], edge_sem.at[3], (prv, tp))
    tail.start()

    flip_s = flip().astype(BF16)

    def filter_sums(c, carry):
        for n in range(2):
            own_rows = jnp.dot(
                flip_s, gmix[c, n * HALF : (n + 1) * HALF, :], preferred_element_type=F32
            ).astype(BF16)
            for g in range(per_tile):
                keep = (lane_group == g).astype(BF16)
                lhs_s[g * HALF : (g + 1) * HALF, :] = own_rows * keep
            big[n] = lax.dot_general(
                lhs_s[...],
                prod[c, n * HALF : n * HALF + ROWS, :],
                (((1,), (1,)), ((), ())),
                preferred_element_type=F32,
            )
        lines = []
        for g in range(per_tile):
            rows = slice(g * HALF, (g + 1) * HALF)
            folded = jnp.zeros((HALF, LANES), F32)
            for n in range(2):
                folded += big[n, rows, 0:LANES] * fmask32[n, :, 0:LANES]
                folded += big[n, rows, LANES:] * fmask32[n, :, LANES:]
            turned = pltpu.roll(folded, 0, 1, stride=1, stride_axis=0)
            lines.append(jnp.sum(turned, axis=0, keepdims=True))
        lines = jnp.concatenate(lines, axis=0)
        red[c, 0:per_tile, :] = jnp.dot(
            lines, flip().astype(F32), preferred_element_type=F32, precision=lax.Precision.HIGHEST
        )
        return carry

    lax.fori_loop(0, nt, filter_sums, 0)
    backward_conv(1)
    tail.wait_recv()

    def finish(c, carry):
        for a in range(3):
            grads[a, c, ROWS : ROWS + 2, :] = tail_r[2 * a : 2 * a + 2, cols(c)]
            w = wsc[c, a]
            sums3 = [jnp.zeros((1, LANES), F32) for _ in range(SHORT)]
            for start in (0, HALF):
                x = xf[a, c, 8 + start : 8 + start + HALF, :]
                h0 = grads[a, c, start : start + HALF, :]
                h1 = grads[a, c, start + 1 : start + 1 + HALF, :] * m1[start + 1 : start + 1 + HALF, :]
                h2 = grads[a, c, start + 2 : start + 2 + HALF, :] * m2[start + 2 : start + 2 + HALF, :]
                value = w[0:1] * h0 + w[1:2] * h1 + w[2:3] * h2
                outs[a, start : start + HALF, cols(c)] = value.astype(BF16)
                for j, h in enumerate((h0, h1, h2)):
                    sums3[j] += jnp.sum(h * x, axis=0, keepdims=True)
            for j in range(SHORT):
                at = 8 + 3 * a + j
                red[c, at : at + 1, :] = sums3[j]
        red[c, 18:24, :] = jnp.zeros((6, LANES), F32)
        return carry

    lax.fori_loop(0, nt, finish, 0)
    stores = [
        pltpu.make_async_copy(outs.at[a], target, store_sem.at[a])
        for a, target in enumerate((gq_hbm, gk_hbm, gv_hbm))
    ]
    for store in stores:
        store.start()

    sends_a = [
        remote(red.at[z_peer(d)], red_a.at[d], ra_send.at[d], ra_recv.at[d], (y_at * nz + z_peer(d), tp))
        for d in range(1, nz)
    ]
    for send in sends_a:
        send.start()
    part = red[z_at]
    for d in range(1, nz):
        sends_a[d - 1].wait_recv()
        part = part + red_a[d]
    red_b[y_at] = part
    sends_b = [
        remote(red_b.at[y_at], red_b.at[y_at], rb_send.at[d], rb_recv.at[d], (y_peer(d) * nz + z_at, tp))
        for d in range(1, ny)
    ]
    for send in sends_b:
        send.start()
    for d in range(1, ny):
        came = red_b.at[y_peer(ny - d)]
        remote(came, came, rb_send.at[d], rb_recv.at[d], (y_peer(d) * nz + z_at, tp)).wait_recv()
    whole = red_b[0]
    for p in range(1, ny):
        whole = whole + red_b[p]
    fin[z_at] = whole * grad_scale
    sends_c = [
        remote(fin.at[z_at], fin.at[z_at], rc_send.at[d], rc_recv.at[d], (y_at * nz + z_peer(d), tp))
        for d in range(1, nz)
    ]
    for send in sends_c:
        send.start()
    for d in range(1, nz):
        came = fin.at[z_peer(nz - d)]
        remote(came, came, rc_send.at[d], rc_recv.at[d], (y_at * nz + z_peer(d), tp)).wait_recv()
    for c in range(nt):
        span = slice(c * LANES, (c + 1) * LANES)
        filt_out[c * per_tile : (c + 1) * per_tile, :] = fin[c, 0:per_tile, :]
        gain_out[:, span] = fin[c, 17:18, :]
        for a in range(3):
            short_out[a, :, span] = fin[c, 8 + 3 * a : 11 + 3 * a, :]

    for copy in [doc_fwd, doc_bwd, edge, tail] + sends + sends_a + sends_b + sends_c:
        copy.wait_send()

    def drain(c, carry):
        halo1(c).wait_send()
        halo2(c).wait_send()
        return carry

    lax.fori_loop(0, nt, drain, 0)
    for store in stores:
        store.wait()


def on_device(nz, q_in, k_in, v_in, grad_out, doc_ids, gain, filters, short_weight):
    rows, channels = q_in.shape
    groups, taps = filters.shape
    ntp = lax.axis_size("tp")
    ny = lax.axis_size("ctx") // nz
    nt = channels // LANES
    assert rows == ROWS and taps == HALF and nt == nz and groups == 8 * nt
    hbm = pl.BlockSpec(memory_space=pl.ANY)
    vmem = pl.BlockSpec(memory_space=pltpu.VMEM)
    tall = jax.ShapeDtypeStruct((rows, channels), BF16)
    dma = pltpu.SemaphoreType.DMA
    out = pl.pallas_call(
        functools.partial(kernel, ny, nz, ntp),
        name="mixer_backward",
        out_shape=(
            tall,
            tall,
            tall,
            jax.ShapeDtypeStruct((1, channels), F32),
            jax.ShapeDtypeStruct((groups, taps), F32),
            jax.ShapeDtypeStruct((3, SHORT, channels), F32),
        ),
        in_specs=[hbm] * 4 + [vmem] * 4,
        out_specs=(hbm, hbm, hbm, vmem, vmem, vmem),
        scratch_shapes=[
            pltpu.VMEM((3, rows, channels), BF16),
            pltpu.VMEM((rows, channels), BF16),
            pltpu.VMEM((3, nt, rows + 8, LANES), F32),
            pltpu.VMEM((3, nt, rows, LANES), F32),
            pltpu.VMEM((nt, rows, LANES), F32),
            pltpu.VMEM((nt, rows, LANES), F32),
            pltpu.VMEM((3, nt, rows + 8, LANES), F32),
            pltpu.VMEM((3, rows, channels), BF16),
            pltpu.VMEM((nt, rows + HALF, LANES), BF16),
            pltpu.VMEM((nt, rows + HALF, LANES), BF16),
            pltpu.VMEM((2, nt, 8 * HALF, 2 * LANES), BF16),
            pltpu.VMEM((2, nt, 8 * HALF, 2 * LANES), BF16),
            pltpu.VMEM((2, HALF, 2 * LANES), BF16),
            pltpu.VMEM((2, HALF, 2 * LANES), BF16),
            pltpu.VMEM((2, HALF, 2 * LANES), F32),
            pltpu.VMEM((groups, LANES), F32),
            pltpu.VMEM((groups, LANES), F32),
            pltpu.VMEM((nt, 4, 8, LANES), F32),
            pltpu.VMEM((rows + 16, LANES), F32),
            pltpu.VMEM((rows + 8, LANES), F32),
            pltpu.VMEM((rows + 8, LANES), F32),
            pltpu.VMEM((2, LANES), jnp.int32),
            pltpu.VMEM((2, LANES), jnp.int32),
            pltpu.VMEM((8, channels), F32),
            pltpu.VMEM((8, channels), F32),
            pltpu.VMEM((8, channels), F32),
            pltpu.VMEM((8, channels), F32),
            pltpu.VMEM((2, 2, HALF, LANES), F32),
            pltpu.VMEM((ntp, 8, LANES), F32),
            pltpu.VMEM((2, 2, HALF, LANES), F32),
            pltpu.VMEM((2, 8 * HALF, 2 * LANES), F32),
            pltpu.VMEM((8 * HALF, LANES), F32),
            pltpu.VMEM((8 * HALF, LANES), BF16),
            pltpu.VMEM((nt, CHUNK, LANES), F32),
            pltpu.VMEM((nz, CHUNK, LANES), F32),
            pltpu.VMEM((ny, CHUNK, LANES), F32),
            pltpu.VMEM((nz, CHUNK, LANES), F32),
            dma((4,)),
            dma((3,)),
            dma((4,)),
            dma((4,)),
            dma((nt,)),
            dma((nt,)),
            dma((nt,)),
            dma((nt,)),
            dma((ntp,)),
            dma((ntp,)),
            dma((nz,)),
            dma((nz,)),
            dma((ny,)),
            dma((ny,)),
            dma((nz,)),
            dma((nz,)),
        ],
        compiler_params=pltpu.CompilerParams(
            collective_id=0, has_side_effects=True, vmem_limit_bytes=60 * 1024 * 1024
        ),
    )(
        q_in,
        k_in,
        v_in,
        grad_out,
        doc_ids.reshape(2, LANES),
        gain.reshape(1, channels),
        filters,
        short_weight,
    )
    return out[0], out[1], out[2], out[3].reshape(channels), out[4], out[5]


def solution(mesh, ring=RING):
    return jax.shard_map(
        functools.partial(on_device, ring),
        mesh=mesh,
        in_specs=(
            P("ctx", "tp"),
            P("ctx", "tp"),
            P("ctx", "tp"),
            P("ctx", "tp"),
            P("ctx"),
            P("tp"),
            P("tp", None),
            P(None, None, "tp"),
        ),
        out_specs=(
            P("ctx", "tp"),
            P("ctx", "tp"),
            P("ctx", "tp"),
            P("tp"),
            P("tp", None),
            P(None, None, "tp"),
        ),
        check_vma=False,
    )
```

```python
import functools
import math

import jax
import jax.numpy as jnp
from jax import lax
from jax.experimental import pallas as pl
from jax.experimental.pallas import tpu as pltpu
from jax.sharding import PartitionSpec as P

F32 = jnp.float32
BF16 = jnp.bfloat16
MESH = pl.DeviceIdType.MESH
LANES = 128
HALF = 128
ROWS = 256
SHORT = 3
EPS = 1e-06
RING = 8
CHUNK = 24


def iota(axis):
    return lax.broadcasted_iota(jnp.int32, (LANES, LANES), axis)


def as_column(row):
    eye = iota(0) == iota(1)
    spread = jnp.where(eye, jnp.broadcast_to(row, (LANES, LANES)), 0.0)
    return jnp.sum(spread, axis=1, keepdims=True)


def flip():
    return iota(0) + iota(1) == LANES - 1


def mirror():
    total = iota(0) + iota(1)
    return jnp.where((total == 0) | (total == LANES), 1.0, 0.0)


def kernel(
    ny,
    nz,
    ntp,
    q_hbm,
    k_hbm,
    v_hbm,
    go_hbm,
    docs_ref,
    gain_ref,
    filt_ref,
    sw_ref,
    gq_ref,
    gk_ref,
    gv_ref,
    gain_out,
    filt_out,
    short_out,
    xin,
    go_v,
    xf,
    feats,
    mixed,
    y_s,
    grads,
    prod,
    gmix,
    ring_f,
    ring_b,
    fmask,
    bmask,
    fmask32,
    filt32,
    filt_rev,
    wsc,
    dcol,
    m1,
    m2,
    docs_prev,
    docs_next,
    edge_s,
    edge_r,
    tail_s,
    tail_r,
    acc,
    stats,
    scales,
    big,
    small,
    lhs_s,
    turned_s,
    red,
    red_a,
    red_b,
    fin,
    load_sem,
    doc_sem,
    edge_sem,
    h1_send,
    h1_recv,
    h2_send,
    h2_recv,
    st_send,
    st_recv,
    ra_send,
    ra_recv,
    rb_send,
    rb_recv,
    rc_send,
    rc_recv,
):
    nt = nz
    outs = (gq_ref, gk_ref, gv_ref)
    groups = filt_ref.shape[0]
    per_tile = groups // nt
    width = LANES // per_tile
    n_ctx = ny * nz
    channels = nt * LANES
    total_channels = channels * ntp
    grad_scale = 1.0 / math.sqrt(ROWS * n_ctx)
    ctx = lax.axis_index("ctx")
    tp = lax.axis_index("tp")
    nxt = lax.rem(ctx + 1, n_ctx)
    prv = lax.rem(ctx + n_ctx - 1, n_ctx)
    y_at = lax.div(ctx, nz)
    z_at = lax.rem(ctx, nz)

    def z_peer(d):
        return lax.rem(z_at + d, nz)

    def y_peer(d):
        return lax.rem(y_at + d, ny)

    def tp_peer(d):
        return lax.rem(tp + d, ntp)

    def remote(src, dst, send, recv, where):
        return pltpu.make_async_remote_copy(
            src_ref=src, dst_ref=dst, send_sem=send, recv_sem=recv, device_id=where, device_id_type=MESH
        )

    loads = [
        pltpu.make_async_copy(k_hbm, xin.at[1], load_sem.at[1]),
        pltpu.make_async_copy(v_hbm, xin.at[2], load_sem.at[2]),
        pltpu.make_async_copy(q_hbm, xin.at[0], load_sem.at[0]),
        pltpu.make_async_copy(go_hbm, go_v, load_sem.at[3]),
    ]
    for load in loads:
        load.start()

    barrier = pltpu.get_barrier_semaphore()
    partners = [(nxt, tp), (prv, tp)]
    partners += [(ctx, tp_peer(d)) for d in range(1, ntp)]
    partners += [(y_at * nz + z_peer(d), tp) for d in range(1, nz)]
    partners += [(y_peer(d) * nz + z_at, tp) for d in range(1, ny)]
    for where in partners:
        pl.semaphore_signal(barrier, inc=1, device_id=where, device_id_type=MESH)

    for a in range(3):
        taps = sw_ref[a].astype(F32)
        for c in range(nt):
            wsc[c, a, 0:SHORT, :] = taps[:, c * LANES : (c + 1) * LANES]
    for c in range(nt):
        wsc[c, 3, 0:1, :] = gain_ref[c * LANES : (c + 1) * LANES].astype(F32).reshape(1, LANES)
    filt32[...] = filt_ref[...].astype(F32)
    filt_rev[...] = jnp.dot(filt_ref[...], mirror().astype(BF16), preferred_element_type=F32)

    docs_f = docs_ref[...].astype(F32)
    own = [docs_f[0:1], docs_f[1:2]]
    own_col = [as_column(row) for row in own]
    for n in range(2):
        dcol[8 + HALF * n : 8 + HALF * (n + 1), :] = jnp.broadcast_to(own_col[n], (HALF, LANES))

    def short_masks(start, size):
        here = dcol[8 + start : 8 + start + size, :]
        m1[start : start + size, :] = (dcol[7 + start : 7 + start + size, :] == here).astype(F32)
        m2[start : start + size, :] = (dcol[6 + start : 6 + start + size, :] == here).astype(F32)

    short_masks(HALF, HALF)

    for load in loads[:3]:
        load.wait()
    for a in range(3):
        last = xin[a, ROWS - 16 : ROWS, :].astype(F32)
        edge_s[2 * a : 2 * a + 2, :] = last[14:16]
    edge_s[6:8, :] = jnp.zeros((2, channels), F32)

    pl.semaphore_wait(barrier, len(partners))

    doc_fwd = remote(docs_ref, docs_prev, doc_sem.at[0], doc_sem.at[1], (nxt, tp))
    doc_bwd = remote(docs_ref, docs_next, doc_sem.at[2], doc_sem.at[3], (prv, tp))
    edge = remote(edge_s, edge_r, edge_sem.at[0], edge_sem.at[1], (nxt, tp))
    doc_fwd.start()
    doc_bwd.start()
    edge.start()

    def cols(c):
        return pl.ds(pl.multiple_of(c * LANES, LANES), LANES)

    def feature(a, c, start):
        x0 = xf[a, c, pl.ds(8 + start, HALF), :]
        x1 = xf[a, c, pl.ds(7 + start, HALF), :]
        x2 = xf[a, c, pl.ds(6 + start, HALF), :]
        w = wsc[c, a]
        return (
            w[0:1] * x0
            + w[1:2] * x1 * m1[start : start + HALF, :]
            + w[2:3] * x2 * m2[start : start + HALF, :]
        )

    def halo1(c):
        return remote(
            prod.at[c, pl.ds(ROWS, HALF)], prod.at[c, pl.ds(0, HALF)], h1_send.at[c], h1_recv.at[c], (nxt, tp)
        )

    def halo2(c):
        return remote(
            gmix.at[c, pl.ds(0, HALF)], gmix.at[c, pl.ds(ROWS, HALF)], h2_send.at[c], h2_recv.at[c], (prv, tp)
        )

    def products(c, start):
        fk = feature(1, c, start)
        fv = feature(2, c, start)
        feats[1, c, start : start + HALF, :] = fk
        feats[2, c, start : start + HALF, :] = fv
        prod[c, HALF + start : 2 * HALF + start, :] = (fk * fv).astype(BF16)

    def late_half(c, carry):
        for a in (1, 2):
            xf[a, c, 8 : 8 + ROWS, :] = xin[a, :, cols(c)].astype(F32)
        products(c, HALF)
        halo1(c).start()
        return carry

    lax.fori_loop(0, nt, late_half, 0)

    def build(source, target):
        def one(c, carry):
            rows = source[pl.ds(pl.multiple_of(c * per_tile, per_tile), per_tile), :]
            for g in range(per_tile):
                row = jnp.broadcast_to(rows[g : g + 1], (HALF, LANES))
                band = pltpu.roll(row, 0, 1, stride=1, stride_axis=0)
                target[c, g * HALF : (g + 1) * HALF, :] = band.astype(BF16)
            return carry

        lax.fori_loop(0, nt, one, 0)

    build(filt_rev, ring_f)

    doc_fwd.wait_recv()
    doc_bwd.wait_recv()
    edge.wait_recv()
    row_prev = jnp.where(ctx == 0, -1.0, docs_prev[1:2, :].astype(F32))
    row_next = jnp.where(ctx == n_ctx - 1, -1.0, docs_next[0:1, :].astype(F32))
    col_prev = as_column(row_prev)
    col_next = as_column(row_next)
    dcol[0:8, :] = jnp.broadcast_to(col_prev[HALF - 8 :], (8, LANES))
    dcol[8 + ROWS : 16 + ROWS, :] = jnp.broadcast_to(col_next[:8], (8, LANES))
    short_masks(0, HALF)
    short_masks(ROWS, 8)
    i_at, j_at = iota(0), iota(1)

    def pick(keep, column, row):
        return jnp.where(keep & (column == row), 1.0, 0.0)

    flip_s = flip().astype(BF16)
    before_rows = (row_prev, own[0])
    after_rows = (own[1], row_next)
    for n in range(2):
        fmask[n, 0] = pick(j_at > i_at, own_col[n], before_rows[n]).astype(BF16)
        fmask[n, 1] = pick(j_at <= i_at, own_col[n], own[n]).astype(BF16)
        for side in range(2):
            fmask32[n, side] = jnp.dot(fmask[n, side], flip_s, preferred_element_type=F32)
        bmask[n, 0] = pick(j_at >= i_at, own_col[n], own[n]).astype(BF16)
        bmask[n, 1] = pick(j_at < i_at, own_col[n], after_rows[n]).astype(BF16)

    def early_half(c, carry):
        xf[0, c, 8 : 8 + ROWS, :] = xin[0, :, cols(c)].astype(F32)
        for a in range(3):
            xf[a, c, 6:8, :] = edge_r[2 * a : 2 * a + 2, cols(c)]
        products(c, 0)
        for start in (0, HALF):
            feats[0, c, start : start + HALF, :] = feature(0, c, start)
        return carry

    lax.fori_loop(0, nt, early_half, 0)
    loads[3].wait()

    lane_group = lax.div(iota(1), width)

    def convolve(bands, masks, window, slot):
        for g in range(per_tile):
            rows = slice(g * HALF, (g + 1) * HALF)
            band = bands[rows, :]
            for side in range(2):
                lhs_s[slot, side, rows, :] = band * masks[side]
        lhs = jnp.concatenate([lhs_s[slot, 0], lhs_s[slot, 1]], axis=1)
        small[slot] = jnp.dot(lhs, window, preferred_element_type=F32)
        value = small[slot, 0:HALF, :]
        for g in range(1, per_tile):
            value = jnp.where(lane_group == g, small[slot, g * HALF : (g + 1) * HALF, :], value)
        return value

    def tiles(body, ready=None, unroll=2):
        def step(i, carry):
            if ready is not None:
                for u in range(unroll):
                    ready(i * unroll + u)
            for u in range(unroll):
                body(i * unroll + u, u)
            return carry

        lax.fori_loop(0, nt // unroll, step, 0)

    acc[...] = jnp.zeros_like(acc)

    def forward(n):
        span = slice(n * HALF, (n + 1) * HALF)

        def one(c, slot):
            value = convolve(ring_f.at[c], fmask[n], prod[c, n * HALF : n * HALF + ROWS, :], slot)
            mixed[c, span, :] = value
            y = feats[0, c, span, :] * value
            y_s[c, span, :] = y
            weighted = wsc[c, 3, 0:1, :] * go_v[span, cols(c)].astype(F32)
            acc[n, 0] += y * y
            acc[n, 1] += weighted * y

        tiles(one, (lambda c: halo1(c).wait_recv()) if n == 0 else None)

    forward(1)
    forward(0)

    stats[tp] = jnp.zeros((8, LANES), F32)
    for n in range(2):
        for kind in range(2):
            line = jnp.sum(acc[n, kind].T, axis=0, keepdims=True)
            stats[tp, 2 * kind + n : 2 * kind + n + 1, :] = line
    sends = [
        remote(stats.at[tp], stats.at[tp], st_send.at[d], st_recv.at[d], (ctx, tp_peer(d)))
        for d in range(1, ntp)
    ]
    for send in sends:
        send.start()
    build(filt32, ring_b)
    for d in range(1, ntp):
        came = stats.at[tp_peer(ntp - d)]
        remote(came, came, st_send.at[d], st_recv.at[d], (ctx, tp_peer(d))).wait_recv()
    sums = stats[0]
    for p in range(1, ntp):
        sums = sums + stats[p]
    scale = lax.rsqrt(sums[0:2] / total_channels + EPS)
    pull = scale * scale * scale * sums[2:4] / total_channels
    for n in range(2):
        scales[n, 0] = jnp.broadcast_to(as_column(scale[n : n + 1]), (HALF, LANES))
        scales[n, 1] = jnp.broadcast_to(as_column(pull[n : n + 1]), (HALF, LANES))

    def backward_norm(n):
        span = slice(n * HALF, (n + 1) * HALF)

        def one(c, carry):
            cot = go_v[span, cols(c)].astype(F32)
            y = y_s[c, span, :]
            row_scale = scales[n, 0]
            grad_y = row_scale * (wsc[c, 3, 0:1, :] * cot) - y * scales[n, 1]
            gain_part = jnp.sum(cot * y * row_scale, axis=0, keepdims=True)
            if n == 0:
                red[c, 17:18, :] = gain_part
            else:
                red[c, 17:18, :] += gain_part
            gmix[c, span, :] = (grad_y * feats[0, c, span, :]).astype(BF16)
            if n == 0:
                halo2(c).start()
            grads[0, c, span, :] = grad_y * mixed[c, span, :]
            if n == 0:
                tail_s[0:2, cols(c)] = grads[0, c, 0:2, :]
            return carry

        lax.fori_loop(0, nt, one, 0)

    backward_norm(0)
    backward_norm(1)

    def backward_conv(n):
        span = slice(n * HALF, (n + 1) * HALF)

        def one(c, slot):
            value = convolve(ring_b.at[c], bmask[n], gmix[c, n * HALF : n * HALF + ROWS, :], slot)
            grads[1, c, span, :] = value * feats[2, c, span, :]
            grads[2, c, span, :] = value * feats[1, c, span, :]
            if n == 0:
                tail_s[2:4, cols(c)] = grads[1, c, 0:2, :]
                tail_s[4:6, cols(c)] = grads[2, c, 0:2, :]

        tiles(one, (lambda c: halo2(c).wait_recv()) if n == 1 else None)

    tail_s[6:8, :] = jnp.zeros((2, channels), F32)
    backward_conv(0)
    tail = remote(tail_s, tail_r, edge_sem.at[2], edge_sem.at[3], (prv, tp))
    tail.start()

    def filter_sums(c, carry):
        for at in range(3):
            block = prod[c, at * HALF : (at + 1) * HALF, :]
            turned_s[at] = jnp.dot(flip_s, block, preferred_element_type=F32).astype(BF16)
        for n in range(2):
            own_rows = gmix[c, n * HALF : (n + 1) * HALF, :]
            for g in range(per_tile):
                keep = (lane_group == g).astype(BF16)
                lhs_s[n, 0, g * HALF : (g + 1) * HALF, :] = own_rows * keep
            window = jnp.concatenate([turned_s[n], turned_s[n + 1]], axis=0)
            big[n] = lax.dot_general(
                lhs_s[n, 0], window, (((1,), (1,)), ((), ())), preferred_element_type=F32
            )
        for g in range(per_tile):
            rows = slice(g * HALF, (g + 1) * HALF)
            folded = jnp.zeros((HALF, LANES), F32)
            for n in range(2):
                folded += big[n, rows, 0:LANES] * fmask32[n, 0]
                folded += big[n, rows, LANES:] * fmask32[n, 1]
            turned = pltpu.roll(folded, 1, 1, stride=1, stride_axis=0)
            red[c, g : g + 1, :] = jnp.sum(turned, axis=0, keepdims=True)
        return carry

    lax.fori_loop(0, nt, filter_sums, 0)
    backward_conv(1)
    tail.wait_recv()

    def finish(c, carry):
        for a in range(3):
            grads[a, c, ROWS : ROWS + 2, :] = tail_r[2 * a : 2 * a + 2, cols(c)]
            w = wsc[c, a]
            sums3 = [jnp.zeros((1, LANES), F32) for _ in range(SHORT)]
            for start in (0, HALF):
                x = xf[a, c, 8 + start : 8 + start + HALF, :]
                h0 = grads[a, c, start : start + HALF, :]
                h1 = grads[a, c, start + 1 : start + 1 + HALF, :] * m1[start + 1 : start + 1 + HALF, :]
                h2 = grads[a, c, start + 2 : start + 2 + HALF, :] * m2[start + 2 : start + 2 + HALF, :]
                value = w[0:1] * h0 + w[1:2] * h1 + w[2:3] * h2
                outs[a][start : start + HALF, cols(c)] = value.astype(BF16)
                for j, h in enumerate((h0, h1, h2)):
                    sums3[j] += jnp.sum(h * x, axis=0, keepdims=True)
            for j in range(SHORT):
                at = 8 + 3 * a + j
                red[c, at : at + 1, :] = sums3[j]
        red[c, 18:24, :] = jnp.zeros((6, LANES), F32)
        return carry

    lax.fori_loop(0, nt, finish, 0)
    sends_a = [
        remote(red.at[z_peer(d)], red_a.at[d], ra_send.at[d], ra_recv.at[d], (y_at * nz + z_peer(d), tp))
        for d in range(1, nz)
    ]
    for send in sends_a:
        send.start()
    part = red[z_at]
    for d in range(1, nz):
        sends_a[d - 1].wait_recv()
        part = part + red_a[d]
    red_b[y_at] = part
    sends_b = [
        remote(red_b.at[y_at], red_b.at[y_at], rb_send.at[d], rb_recv.at[d], (y_peer(d) * nz + z_at, tp))
        for d in range(1, ny)
    ]
    for send in sends_b:
        send.start()
    for d in range(1, ny):
        came = red_b.at[y_peer(ny - d)]
        remote(came, came, rb_send.at[d], rb_recv.at[d], (y_peer(d) * nz + z_at, tp)).wait_recv()
    whole = red_b[0]
    for p in range(1, ny):
        whole = whole + red_b[p]
    fin[z_at] = whole * grad_scale
    sends_c = [
        remote(fin.at[z_at], fin.at[z_at], rc_send.at[d], rc_recv.at[d], (y_at * nz + z_peer(d), tp))
        for d in range(1, nz)
    ]
    for send in sends_c:
        send.start()
    for d in range(1, nz):
        came = fin.at[z_peer(nz - d)]
        remote(came, came, rc_send.at[d], rc_recv.at[d], (y_at * nz + z_peer(d), tp)).wait_recv()
    for c in range(nt):
        span = slice(c * LANES, (c + 1) * LANES)
        filt_out[c * per_tile : (c + 1) * per_tile, :] = fin[c, 0:per_tile, :]
        gain_out[:, span] = fin[c, 17:18, :]
        for a in range(3):
            short_out[a, :, span] = fin[c, 8 + 3 * a : 11 + 3 * a, :]

    for copy in [doc_fwd, doc_bwd, edge, tail] + sends + sends_a + sends_b + sends_c:
        copy.wait_send()

    def drain(c, carry):
        halo1(c).wait_send()
        halo2(c).wait_send()
        return carry

    lax.fori_loop(0, nt, drain, 0)


def resident(shape, dtype):
    return pltpu.VMEM(shape, dtype)


def pinned(value):
    return pltpu.with_memory_space_constraint(value, pltpu.VMEM)


def publish(*refs):
    count = (len(refs) - 1) // 2
    sem = refs[-1]
    copies = [pltpu.make_async_copy(refs[i], refs[count + i], sem.at[i]) for i in range(count)]
    for copy in copies:
        copy.start()
    for copy in copies:
        copy.wait()


def on_device(nz, q_in, k_in, v_in, grad_out, doc_ids, gain, filters, short_weight):
    rows, channels = q_in.shape
    groups, taps = filters.shape
    ntp = lax.axis_size("tp")
    ny = lax.axis_size("ctx") // nz
    nt = channels // LANES
    assert rows == ROWS and taps == HALF and nt == nz and groups == 8 * nt
    hbm = pl.BlockSpec(memory_space=pl.ANY)
    vmem = pl.BlockSpec(memory_space=pltpu.VMEM)
    tall = resident((rows, channels), BF16)
    dma = pltpu.SemaphoreType.DMA
    held = pl.pallas_call(
        functools.partial(kernel, ny, nz, ntp),
        name="mixer_backward",
        out_shape=(
            tall,
            tall,
            tall,
            resident((1, channels), F32),
            resident((groups, taps), F32),
            resident((3, SHORT, channels), F32),
        ),
        in_specs=[pl.BlockSpec(memory_space=pltpu.HBM)] * 4 + [vmem] * 4,
        out_specs=(vmem,) * 6,
        scratch_shapes=[
            pltpu.VMEM((3, rows, channels), BF16),
            pltpu.VMEM((rows, channels), BF16),
            pltpu.VMEM((3, nt, rows + 8, LANES), F32),
            pltpu.VMEM((3, nt, rows, LANES), F32),
            pltpu.VMEM((nt, rows, LANES), F32),
            pltpu.VMEM((nt, rows, LANES), F32),
            pltpu.VMEM((3, nt, rows + 8, LANES), F32),
            pltpu.VMEM((nt, rows + HALF, LANES), BF16),
            pltpu.VMEM((nt, rows + HALF, LANES), BF16),
            pltpu.VMEM((nt, 8 * HALF, LANES), BF16),
            pltpu.VMEM((nt, 8 * HALF, LANES), BF16),
            pltpu.VMEM((2, 2, HALF, LANES), BF16),
            pltpu.VMEM((2, 2, HALF, LANES), BF16),
            pltpu.VMEM((2, 2, HALF, LANES), F32),
            pltpu.VMEM((groups, LANES), F32),
            pltpu.VMEM((groups, LANES), F32),
            pltpu.VMEM((nt, 4, 8, LANES), F32),
            pltpu.VMEM((rows + 16, LANES), F32),
            pltpu.VMEM((rows + 8, LANES), F32),
            pltpu.VMEM((rows + 8, LANES), F32),
            pltpu.VMEM((2, LANES), jnp.int32),
            pltpu.VMEM((2, LANES), jnp.int32),
            pltpu.VMEM((8, channels), F32),
            pltpu.VMEM((8, channels), F32),
            pltpu.VMEM((8, channels), F32),
            pltpu.VMEM((8, channels), F32),
            pltpu.VMEM((2, 2, HALF, LANES), F32),
            pltpu.VMEM((ntp, 8, LANES), F32),
            pltpu.VMEM((2, 2, HALF, LANES), F32),
            pltpu.VMEM((2, 8 * HALF, 2 * LANES), F32),
            pltpu.VMEM((2, 8 * HALF, LANES), F32),
            pltpu.VMEM((2, 2, 8 * HALF, LANES), BF16),
            pltpu.VMEM((3, HALF, LANES), BF16),
            pltpu.VMEM((nt, CHUNK, LANES), F32),
            pltpu.VMEM((nz, CHUNK, LANES), F32),
            pltpu.VMEM((ny, CHUNK, LANES), F32),
            pltpu.VMEM((nz, CHUNK, LANES), F32),
            dma((4,)),
            dma((4,)),
            dma((4,)),
            dma((nt,)),
            dma((nt,)),
            dma((nt,)),
            dma((nt,)),
            dma((ntp,)),
            dma((ntp,)),
            dma((nz,)),
            dma((nz,)),
            dma((ny,)),
            dma((ny,)),
            dma((nz,)),
            dma((nz,)),
        ],
        compiler_params=pltpu.CompilerParams(
            collective_id=0, has_side_effects=True, vmem_limit_bytes=60 * 1024 * 1024
        ),
    )(
        q_in,
        k_in,
        v_in,
        grad_out,
        doc_ids.reshape(2, LANES),
        gain,
        filters,
        short_weight,
    )
    out = pl.pallas_call(
        publish,
        name="publish",
        out_shape=[jax.ShapeDtypeStruct(x.shape, x.dtype) for x in held],
        in_specs=[vmem] * 6,
        out_specs=[hbm] * 6,
        scratch_shapes=[dma((6,))],
    )(*[pinned(x) for x in held])
    return out[0], out[1], out[2], out[3].reshape(channels), out[4], out[5]


def solution(mesh, ring=RING):
    return jax.shard_map(
        functools.partial(on_device, ring),
        mesh=mesh,
        in_specs=(
            P("ctx", "tp"),
            P("ctx", "tp"),
            P("ctx", "tp"),
            P("ctx", "tp"),
            P("ctx"),
            P("tp"),
            P("tp", None),
            P(None, None, "tp"),
        ),
        out_specs=(
            P("ctx", "tp"),
            P("ctx", "tp"),
            P("ctx", "tp"),
            P("tp"),
            P("tp", None),
            P(None, None, "tp"),
        ),
        check_vma=False,
    )
```

```python
import functools
import math

import jax
import jax.numpy as jnp
from jax import lax
from jax.experimental import pallas as pl
from jax.experimental.pallas import tpu as pltpu
from jax.sharding import PartitionSpec as P

F32 = jnp.float32
BF16 = jnp.bfloat16
MESH = pl.DeviceIdType.MESH
LANES = 128
HALF = 128
ROWS = 256
SHORT = 3
EPS = 1e-06
RING = 8
SPLIT = 120


def iota(axis):
    return lax.broadcasted_iota(jnp.int32, (LANES, LANES), axis)


def as_column(row):
    eye = iota(0) == iota(1)
    spread = jnp.where(eye, jnp.broadcast_to(row, (LANES, LANES)), 0.0)
    return jnp.sum(spread, axis=1, keepdims=True)


def flip():
    return iota(0) + iota(1) == LANES - 1


def mirror():
    total = iota(0) + iota(1)
    return jnp.where((total == 0) | (total == LANES), 1.0, 0.0)


def kernel(
    ny,
    nz,
    ntp,
    q_hbm,
    k_hbm,
    v_hbm,
    go_hbm,
    docs_ref,
    gain_ref,
    filt_ref,
    sw_ref,
    gq_ref,
    gk_ref,
    gv_ref,
    gain_out,
    filt_out,
    short_out,
    xin,
    go_v,
    xf,
    feats,
    mixed,
    y_s,
    grads,
    prod,
    gmix,
    ring_f,
    ring_b,
    fmask,
    bmask,
    fmask32,
    filt32,
    filt_rev,
    wsc,
    dcol,
    m1,
    m2,
    docs_prev,
    docs_next,
    edge_s,
    edge_r,
    tail_s,
    tail_r,
    tail_q_s,
    tail_q_r,
    acc,
    stats,
    scales,
    big,
    small,
    lhs_s,
    mirrored,
    red_e,
    red_l,
    e1,
    e2,
    fin_e,
    l1,
    l2,
    fin_l,
    load_sem,
    doc_sem,
    edge_sem,
    h1_send,
    h1_recv,
    h2_send,
    h2_recv,
    st_send,
    st_recv,
    tq_sem,
    e1_send,
    e1_recv,
    e2_send,
    e2_recv,
    e3_send,
    e3_recv,
    l1_send,
    l1_recv,
    l2_send,
    l2_recv,
    l3_send,
    l3_recv,
):
    nt = nz
    outs = (gq_ref, gk_ref, gv_ref)
    groups = filt_ref.shape[0]
    per_tile = groups // nt
    width = LANES // per_tile
    n_ctx = ny * nz
    channels = nt * LANES
    total_channels = channels * ntp
    grad_scale = 1.0 / math.sqrt(ROWS * n_ctx)
    ctx = lax.axis_index("ctx")
    tp = lax.axis_index("tp")
    nxt = lax.rem(ctx + 1, n_ctx)
    prv = lax.rem(ctx + n_ctx - 1, n_ctx)
    y_at = lax.div(ctx, nz)
    z_at = lax.rem(ctx, nz)

    def z_peer(d):
        return lax.rem(z_at + d, nz)

    def y_peer(d):
        return lax.rem(y_at + d, ny)

    def tp_peer(d):
        return lax.rem(tp + d, ntp)

    def remote(src, dst, send, recv, where):
        return pltpu.make_async_remote_copy(
            src_ref=src, dst_ref=dst, send_sem=send, recv_sem=recv, device_id=where, device_id_type=MESH
        )

    loads = [
        pltpu.make_async_copy(k_hbm, xin.at[1], load_sem.at[1]),
        pltpu.make_async_copy(v_hbm, xin.at[2], load_sem.at[2]),
        pltpu.make_async_copy(q_hbm, xin.at[0], load_sem.at[0]),
        pltpu.make_async_copy(go_hbm, go_v, load_sem.at[3]),
    ]
    for load in loads:
        load.start()

    barrier = pltpu.get_barrier_semaphore()
    partners = [(nxt, tp), (prv, tp)]
    partners += [(ctx, tp_peer(d)) for d in range(1, ntp)]
    partners += [(y_at * nz + z_peer(d), tp) for d in range(1, nz)]
    partners += [(y_peer(d) * nz + z_at, tp) for d in range(1, ny)]
    for where in partners:
        pl.semaphore_signal(barrier, inc=1, device_id=where, device_id_type=MESH)

    for a in range(3):
        taps = sw_ref[a].astype(F32)
        for c in range(nt):
            wsc[c, a, 0:SHORT, :] = taps[:, c * LANES : (c + 1) * LANES]
    for c in range(nt):
        wsc[c, 3, 0:1, :] = gain_ref[c * LANES : (c + 1) * LANES].astype(F32).reshape(1, LANES)
    filt32[...] = filt_ref[...].astype(F32)
    filt_rev[...] = jnp.dot(filt_ref[...], mirror().astype(BF16), preferred_element_type=F32)

    docs_f = docs_ref[...].astype(F32)
    own = [docs_f[0:1], docs_f[1:2]]
    own_col = [as_column(row) for row in own]
    for n in range(2):
        dcol[8 + HALF * n : 8 + HALF * (n + 1), :] = jnp.broadcast_to(own_col[n], (HALF, LANES))

    def short_masks(start, size):
        here = dcol[8 + start : 8 + start + size, :]
        m1[start : start + size, :] = (dcol[7 + start : 7 + start + size, :] == here).astype(F32)
        m2[start : start + size, :] = (dcol[6 + start : 6 + start + size, :] == here).astype(F32)

    short_masks(HALF, HALF)

    for load in loads[:3]:
        load.wait()
    for a in range(3):
        last = xin[a, ROWS - 16 : ROWS, :].astype(F32)
        edge_s[2 * a : 2 * a + 2, :] = last[14:16]
    edge_s[6:8, :] = jnp.zeros((2, channels), F32)

    doc_fwd = remote(docs_ref, docs_prev, doc_sem.at[0], doc_sem.at[1], (nxt, tp))
    doc_bwd = remote(docs_ref, docs_next, doc_sem.at[2], doc_sem.at[3], (prv, tp))
    edge = remote(edge_s, edge_r, edge_sem.at[0], edge_sem.at[1], (nxt, tp))

    def cols(c):
        return pl.ds(pl.multiple_of(c * LANES, LANES), LANES)

    def feature(a, c, start):
        x0 = xf[a, c, pl.ds(8 + start, HALF), :]
        x1 = xf[a, c, pl.ds(7 + start, HALF), :]
        x2 = xf[a, c, pl.ds(6 + start, HALF), :]
        w = wsc[c, a]
        return (
            w[0:1] * x0
            + w[1:2] * x1 * m1[start : start + HALF, :]
            + w[2:3] * x2 * m2[start : start + HALF, :]
        )

    def halo1(c):
        return remote(
            prod.at[c, pl.ds(ROWS, HALF)], prod.at[c, pl.ds(0, HALF)], h1_send.at[c], h1_recv.at[c], (nxt, tp)
        )

    def halo2(c):
        return remote(
            gmix.at[c, pl.ds(0, HALF)], gmix.at[c, pl.ds(ROWS, HALF)], h2_send.at[c], h2_recv.at[c], (prv, tp)
        )

    def products(c, start):
        fk = feature(1, c, start)
        fv = feature(2, c, start)
        feats[1, c, start : start + HALF, :] = fk
        feats[2, c, start : start + HALF, :] = fv
        prod[c, HALF + start : 2 * HALF + start, :] = (fk * fv).astype(BF16)

    def late_half(c, carry):
        for a in (1, 2):
            xf[a, c, 8 : 8 + ROWS, :] = xin[a, :, cols(c)].astype(F32)
        products(c, HALF)
        return carry

    lax.fori_loop(0, nt, late_half, 0)
    pl.semaphore_wait(barrier, len(partners))
    doc_fwd.start()
    doc_bwd.start()
    edge.start()

    def send_product(c, carry):
        halo1(c).start()
        return carry

    lax.fori_loop(0, nt, send_product, 0)

    def build(source, target):
        def one(c, carry):
            rows = source[pl.ds(pl.multiple_of(c * per_tile, per_tile), per_tile), :]
            for g in range(per_tile):
                row = jnp.broadcast_to(rows[g : g + 1], (HALF, LANES))
                band = pltpu.roll(row, 0, 1, stride=1, stride_axis=0)
                target[c, g * HALF : (g + 1) * HALF, :] = band.astype(BF16)
            return carry

        lax.fori_loop(0, nt, one, 0)

    build(filt_rev, ring_f)
    build(filt32, ring_b)

    doc_fwd.wait_recv()
    doc_bwd.wait_recv()
    edge.wait_recv()
    row_prev = jnp.where(ctx == 0, -1.0, docs_prev[1:2, :].astype(F32))
    row_next = jnp.where(ctx == n_ctx - 1, -1.0, docs_next[0:1, :].astype(F32))
    col_prev = as_column(row_prev)
    col_next = as_column(row_next)
    dcol[0:8, :] = jnp.broadcast_to(col_prev[HALF - 8 :], (8, LANES))
    dcol[8 + ROWS : 16 + ROWS, :] = jnp.broadcast_to(col_next[:8], (8, LANES))
    short_masks(0, HALF)
    short_masks(ROWS, 8)
    i_at, j_at = iota(0), iota(1)

    def pick(keep, column, row):
        return jnp.where(keep & (column == row), 1.0, 0.0)

    flip_s = flip().astype(BF16)
    before_rows = (row_prev, own[0])
    after_rows = (own[1], row_next)
    for n in range(2):
        fmask[n, 0] = pick(j_at > i_at, own_col[n], before_rows[n]).astype(BF16)
        fmask[n, 1] = pick(j_at <= i_at, own_col[n], own[n]).astype(BF16)
        for side in range(2):
            fmask32[n, side] = jnp.dot(fmask[n, side], flip_s, preferred_element_type=F32)
        bmask[n, 0] = pick(j_at >= i_at, own_col[n], own[n]).astype(BF16)
        bmask[n, 1] = pick(j_at < i_at, own_col[n], after_rows[n]).astype(BF16)

    def early_half(c, carry):
        xf[0, c, 8 : 8 + ROWS, :] = xin[0, :, cols(c)].astype(F32)
        for a in range(3):
            xf[a, c, 6:8, :] = edge_r[2 * a : 2 * a + 2, cols(c)]
        products(c, 0)
        for start in (0, HALF):
            feats[0, c, start : start + HALF, :] = feature(0, c, start)
        return carry

    lax.fori_loop(0, nt, early_half, 0)
    loads[3].wait()

    lane_group = lax.div(iota(1), width)

    def convolve(bands, masks, window, slot):
        for g in range(per_tile):
            rows = slice(g * HALF, (g + 1) * HALF)
            band = bands[rows, :]
            for side in range(2):
                lhs_s[slot, side, rows, :] = band * masks[side]
        lhs = jnp.concatenate([lhs_s[slot, 0], lhs_s[slot, 1]], axis=1)
        small[slot] = jnp.dot(lhs, window, preferred_element_type=F32)
        value = small[slot, 0:HALF, :]
        for g in range(1, per_tile):
            value = jnp.where(lane_group == g, small[slot, g * HALF : (g + 1) * HALF, :], value)
        return value

    def tiles(body, ready=None, unroll=2):
        def step(i, carry):
            if ready is not None:
                for u in range(unroll):
                    ready(i * unroll + u)
            for u in range(unroll):
                body(i * unroll + u, u)
            return carry

        lax.fori_loop(0, nt // unroll, step, 0)

    acc[...] = jnp.zeros_like(acc)

    def mirror_products(c, carry):
        for at in range(3):
            block = prod[c, at * HALF : (at + 1) * HALF, :]
            mirrored[c, at * HALF : (at + 1) * HALF, :] = jnp.dot(
                flip_s, block, preferred_element_type=F32
            ).astype(BF16)
        return carry

    def forward(n):
        span = slice(n * HALF, (n + 1) * HALF)

        def one(c, slot):
            value = convolve(ring_f.at[c], fmask[n], prod[c, n * HALF : n * HALF + ROWS, :], slot)
            mixed[c, span, :] = value
            y = feats[0, c, span, :] * value
            y_s[c, span, :] = y
            weighted = wsc[c, 3, 0:1, :] * go_v[span, cols(c)].astype(F32)
            acc[n, 0] += y * y
            acc[n, 1] += weighted * y

        tiles(one, (lambda c: halo1(c).wait_recv()) if n == 0 else None)

    forward(1)
    forward(0)

    stats[tp] = jnp.zeros((8, LANES), F32)
    for n in range(2):
        for kind in range(2):
            line = jnp.sum(acc[n, kind].T, axis=0, keepdims=True)
            stats[tp, 2 * kind + n : 2 * kind + n + 1, :] = line
    sends = [
        remote(stats.at[tp], stats.at[tp], st_send.at[d], st_recv.at[d], (ctx, tp_peer(d)))
        for d in range(1, ntp)
    ]
    for send in sends:
        send.start()
    lax.fori_loop(0, nt, mirror_products, 0)
    for d in range(1, ntp):
        came = stats.at[tp_peer(ntp - d)]
        remote(came, came, st_send.at[d], st_recv.at[d], (ctx, tp_peer(d))).wait_recv()
    sums = stats[0]
    for p in range(1, ntp):
        sums = sums + stats[p]
    scale = lax.rsqrt(sums[0:2] / total_channels + EPS)
    pull = scale * scale * scale * sums[2:4] / total_channels
    for n in range(2):
        scales[n, 0] = jnp.broadcast_to(as_column(scale[n : n + 1]), (HALF, LANES))
        scales[n, 1] = jnp.broadcast_to(as_column(pull[n : n + 1]), (HALF, LANES))

    def backward_norm(n):
        span = slice(n * HALF, (n + 1) * HALF)

        def one(c, carry):
            cot = go_v[span, cols(c)].astype(F32)
            y = y_s[c, span, :]
            row_scale = scales[n, 0]
            grad_y = row_scale * (wsc[c, 3, 0:1, :] * cot) - y * scales[n, 1]
            gain_part = jnp.sum(cot * y * row_scale, axis=0, keepdims=True)
            if n == 0:
                red_e[c, 8:9, :] = gain_part
            else:
                red_e[c, 8:9, :] += gain_part
            gmix[c, span, :] = (grad_y * feats[0, c, span, :]).astype(BF16)
            if n == 0:
                halo2(c).start()
            grads[0, c, span, :] = grad_y * mixed[c, span, :]
            if n == 0:
                tail_q_s[0:2, cols(c)] = grads[0, c, 0:2, :]
            return carry

        lax.fori_loop(0, nt, one, 0)

    tail_q_s[2:8, :] = jnp.zeros((6, channels), F32)
    backward_norm(0)
    tail_q = remote(tail_q_s, tail_q_r, tq_sem.at[0], tq_sem.at[1], (prv, tp))
    tail_q.start()
    backward_norm(1)

    def backward_conv(n):
        span = slice(n * HALF, (n + 1) * HALF)

        def one(c, slot):
            value = convolve(ring_b.at[c], bmask[n], gmix[c, n * HALF : n * HALF + ROWS, :], slot)
            grads[1, c, span, :] = value * feats[2, c, span, :]
            grads[2, c, span, :] = value * feats[1, c, span, :]
            if n == 0:
                tail_s[2:4, cols(c)] = grads[1, c, 0:2, :]
                tail_s[4:6, cols(c)] = grads[2, c, 0:2, :]
            else:
                finish_last(c)

        tiles(one, (lambda c: halo2(c).wait_recv()) if n == 1 else None)

    tail_s[0:2, :] = jnp.zeros((2, channels), F32)
    tail_s[6:8, :] = jnp.zeros((2, channels), F32)
    backward_conv(0)
    tail = remote(tail_s, tail_r, edge_sem.at[2], edge_sem.at[3], (prv, tp))
    tail.start()

    def filter_sums(c, slot):
        for n in range(2):
            own_rows = gmix[c, n * HALF : (n + 1) * HALF, :]
            for g in range(per_tile):
                keep = (lane_group == g).astype(BF16)
                lhs_s[slot, n, g * HALF : (g + 1) * HALF, :] = own_rows * keep
            big[slot, n] = lax.dot_general(
                lhs_s[slot, n],
                mirrored[c, n * HALF : n * HALF + ROWS, :],
                (((1,), (1,)), ((), ())),
                preferred_element_type=F32,
            )
        for g in range(per_tile):
            rows = slice(g * HALF, (g + 1) * HALF)
            folded = jnp.zeros((HALF, LANES), F32)
            for n in range(2):
                folded += big[slot, n, rows, 0:LANES] * fmask32[n, 0]
                folded += big[slot, n, rows, LANES:] * fmask32[n, 1]
            turned = pltpu.roll(folded, 1, 1, stride=1, stride_axis=0)
            red_e[c, g : g + 1, :] = jnp.sum(turned, axis=0, keepdims=True)
        red_e[c, 12:16, :] = jnp.zeros((4, LANES), F32)

    def finish_rows(a, c, start, size):
        w = wsc[c, a]
        x = xf[a, c, 8 + start : 8 + start + size, :]
        h0 = grads[a, c, start : start + size, :]
        h1 = grads[a, c, start + 1 : start + 1 + size, :] * m1[start + 1 : start + 1 + size, :]
        h2 = grads[a, c, start + 2 : start + 2 + size, :] * m2[start + 2 : start + 2 + size, :]
        value = w[0:1] * h0 + w[1:2] * h1 + w[2:3] * h2
        outs[a][start : start + size, cols(c)] = value.astype(BF16)
        return [jnp.sum(h * x, axis=0, keepdims=True) for h in (h0, h1, h2)]

    def finish_q(c, carry):
        grads[0, c, ROWS : ROWS + 2, :] = tail_q_r[0:2, cols(c)]
        parts = [finish_rows(0, c, start, HALF) for start in (0, HALF)]
        for j in range(SHORT):
            red_e[c, 9 + j : 10 + j, :] = parts[0][j] + parts[1][j]
        return carry

    def finish_first(c, carry):
        for a in (1, 2):
            parts = finish_rows(a, c, 0, SPLIT)
            for j in range(SHORT):
                red_l[c, 3 * a - 3 + j : 3 * a - 2 + j, :] = parts[j]
        red_l[c, 6:8, :] = jnp.zeros((2, LANES), F32)
        return carry

    def finish_last(c):
        for a in (1, 2):
            grads[a, c, ROWS : ROWS + 2, :] = tail_r[2 * a : 2 * a + 2, cols(c)]
            parts = finish_rows(a, c, SPLIT, ROWS - SPLIT)
            for j in range(SHORT):
                red_l[c, 3 * a - 3 + j : 3 * a - 2 + j, :] += parts[j]

    share = nt // ny

    def tiles_of(at):
        return pl.ds(at * share, share)

    def to_owners(own, came, send, recv):
        return [
            remote(own.at[tiles_of(y_peer(d))], came.at[d], send.at[d], recv.at[d], (y_peer(d) * nz + z_at, tp))
            for d in range(1, ny)
        ]

    def to_z(came, send, recv):
        return [
            remote(came.at[z_at], came.at[z_at], send.at[d], recv.at[d], (y_at * nz + z_peer(d), tp))
            for d in range(1, nz)
        ]

    def to_y(whole, send, recv):
        mine = whole.at[tiles_of(y_at)]
        return [remote(mine, mine, send.at[d], recv.at[d], (y_peer(d) * nz + z_at, tp)) for d in range(1, ny)]

    def launch(copies):
        for copy in copies:
            copy.start()

    def add_owned(own, came, copies, target):
        part = own[tiles_of(y_at)]
        for d in range(1, ny):
            copies[d - 1].wait_recv()
            part = part + came[d]
        target[z_at] = part

    def add_z(came, send, recv, whole):
        for d in range(1, nz):
            slot = came.at[z_peer(nz - d)]
            remote(slot, slot, send.at[d], recv.at[d], (y_at * nz + z_peer(d), tp)).wait_recv()
        part = came[0]
        for p in range(1, nz):
            part = part + came[p]
        whole[tiles_of(y_at)] = part * grad_scale

    def wait_y(whole, send, recv):
        for d in range(1, ny):
            slot = whole.at[tiles_of(y_peer(ny - d))]
            remote(slot, slot, send.at[d], recv.at[d], (y_peer(d) * nz + z_at, tp)).wait_recv()

    tail_q.wait_recv()
    lax.fori_loop(0, nt, finish_q, 0)
    tiles(filter_sums)
    e_owner = to_owners(red_e, e1, e1_send, e1_recv)
    launch(e_owner)
    lax.fori_loop(0, nt, finish_first, 0)
    add_owned(red_e, e1, e_owner, e2)
    e_z = to_z(e2, e2_send, e2_recv)
    launch(e_z)
    tail.wait_recv()
    backward_conv(1)
    l_owner = to_owners(red_l, l1, l1_send, l1_recv)
    launch(l_owner)
    add_z(e2, e2_send, e2_recv, fin_e)
    e_y = to_y(fin_e, e3_send, e3_recv)
    launch(e_y)
    add_owned(red_l, l1, l_owner, l2)
    l_z = to_z(l2, l2_send, l2_recv)
    launch(l_z)
    wait_y(fin_e, e3_send, e3_recv)
    for c in range(nt):
        span = slice(c * LANES, (c + 1) * LANES)
        filt_out[c * per_tile : (c + 1) * per_tile, :] = fin_e[c, 0:per_tile, :]
        gain_out[:, span] = fin_e[c, 8:9, :]
        short_out[0, :, span] = fin_e[c, 9:12, :]
    add_z(l2, l2_send, l2_recv, fin_l)
    l_y = to_y(fin_l, l3_send, l3_recv)
    launch(l_y)
    wait_y(fin_l, l3_send, l3_recv)
    for c in range(nt):
        span = slice(c * LANES, (c + 1) * LANES)
        for a in (1, 2):
            short_out[a, :, span] = fin_l[c, 3 * a - 3 : 3 * a, :]

    for copy in [doc_fwd, doc_bwd, edge, tail_q, tail] + sends + e_owner + e_z + e_y + l_owner + l_z + l_y:
        copy.wait_send()

    def drain(c, carry):
        halo1(c).wait_send()
        halo2(c).wait_send()
        return carry

    lax.fori_loop(0, nt, drain, 0)


def resident(shape, dtype):
    return pltpu.VMEM(shape, dtype)


def pinned(value):
    return pltpu.with_memory_space_constraint(value, pltpu.VMEM)


def publish(*refs):
    count = (len(refs) - 1) // 2
    sem = refs[-1]
    copies = [pltpu.make_async_copy(refs[i], refs[count + i], sem.at[i]) for i in range(count)]
    for copy in copies:
        copy.start()
    for copy in copies:
        copy.wait()


def on_device(nz, q_in, k_in, v_in, grad_out, doc_ids, gain, filters, short_weight):
    rows, channels = q_in.shape
    groups, taps = filters.shape
    ntp = lax.axis_size("tp")
    ny = lax.axis_size("ctx") // nz
    nt = channels // LANES
    assert rows == ROWS and taps == HALF and nt == nz and groups == 8 * nt
    hbm = pl.BlockSpec(memory_space=pl.ANY)
    vmem = pl.BlockSpec(memory_space=pltpu.VMEM)
    tall = resident((rows, channels), BF16)
    dma = pltpu.SemaphoreType.DMA
    held = pl.pallas_call(
        functools.partial(kernel, ny, nz, ntp),
        name="mixer_backward",
        out_shape=(
            tall,
            tall,
            tall,
            resident((1, channels), F32),
            resident((groups, taps), F32),
            resident((3, SHORT, channels), F32),
        ),
        in_specs=[pl.BlockSpec(memory_space=pltpu.HBM)] * 4 + [vmem] * 4,
        out_specs=(vmem,) * 6,
        scratch_shapes=[
            pltpu.VMEM((3, rows, channels), BF16),
            pltpu.VMEM((rows, channels), BF16),
            pltpu.VMEM((3, nt, rows + 8, LANES), F32),
            pltpu.VMEM((3, nt, rows, LANES), F32),
            pltpu.VMEM((nt, rows, LANES), F32),
            pltpu.VMEM((nt, rows, LANES), F32),
            pltpu.VMEM((3, nt, rows + 8, LANES), F32),
            pltpu.VMEM((nt, rows + HALF, LANES), BF16),
            pltpu.VMEM((nt, rows + HALF, LANES), BF16),
            pltpu.VMEM((nt, 8 * HALF, LANES), BF16),
            pltpu.VMEM((nt, 8 * HALF, LANES), BF16),
            pltpu.VMEM((2, 2, HALF, LANES), BF16),
            pltpu.VMEM((2, 2, HALF, LANES), BF16),
            pltpu.VMEM((2, 2, HALF, LANES), F32),
            pltpu.VMEM((groups, LANES), F32),
            pltpu.VMEM((groups, LANES), F32),
            pltpu.VMEM((nt, 4, 8, LANES), F32),
            pltpu.VMEM((rows + 16, LANES), F32),
            pltpu.VMEM((rows + 8, LANES), F32),
            pltpu.VMEM((rows + 8, LANES), F32),
            pltpu.VMEM((2, LANES), jnp.int32),
            pltpu.VMEM((2, LANES), jnp.int32),
            pltpu.VMEM((8, channels), F32),
            pltpu.VMEM((8, channels), F32),
            pltpu.VMEM((8, channels), F32),
            pltpu.VMEM((8, channels), F32),
            pltpu.VMEM((8, channels), F32),
            pltpu.VMEM((8, channels), F32),
            pltpu.VMEM((2, 2, HALF, LANES), F32),
            pltpu.VMEM((ntp, 8, LANES), F32),
            pltpu.VMEM((2, 2, HALF, LANES), F32),
            pltpu.VMEM((2, 2, 8 * HALF, 2 * LANES), F32),
            pltpu.VMEM((2, 8 * HALF, LANES), F32),
            pltpu.VMEM((2, 2, 8 * HALF, LANES), BF16),
            pltpu.VMEM((nt, rows + HALF, LANES), BF16),
            pltpu.VMEM((nt, 16, LANES), F32),
            pltpu.VMEM((nt, 8, LANES), F32),
            pltpu.VMEM((ny, nt // ny, 16, LANES), F32),
            pltpu.VMEM((nz, nt // ny, 16, LANES), F32),
            pltpu.VMEM((nt, 16, LANES), F32),
            pltpu.VMEM((ny, nt // ny, 8, LANES), F32),
            pltpu.VMEM((nz, nt // ny, 8, LANES), F32),
            pltpu.VMEM((nt, 8, LANES), F32),
            dma((4,)),
            dma((4,)),
            dma((4,)),
            dma((nt,)),
            dma((nt,)),
            dma((nt,)),
            dma((nt,)),
            dma((ntp,)),
            dma((ntp,)),
            dma((2,)),
            dma((ny,)),
            dma((ny,)),
            dma((nz,)),
            dma((nz,)),
            dma((ny,)),
            dma((ny,)),
            dma((ny,)),
            dma((ny,)),
            dma((nz,)),
            dma((nz,)),
            dma((ny,)),
            dma((ny,)),
        ],
        compiler_params=pltpu.CompilerParams(
            collective_id=0, has_side_effects=True, vmem_limit_bytes=60 * 1024 * 1024
        ),
    )(
        q_in,
        k_in,
        v_in,
        grad_out,
        doc_ids.reshape(2, LANES),
        gain,
        filters,
        short_weight,
    )
    out = pl.pallas_call(
        publish,
        name="publish",
        out_shape=[jax.ShapeDtypeStruct(x.shape, x.dtype) for x in held],
        in_specs=[vmem] * 6,
        out_specs=[hbm] * 6,
        scratch_shapes=[dma((6,))],
    )(*[pinned(x) for x in held])
    return out[0], out[1], out[2], out[3].reshape(channels), out[4], out[5]


def solution(mesh, ring=RING):
    return jax.shard_map(
        functools.partial(on_device, ring),
        mesh=mesh,
        in_specs=(
            P("ctx", "tp"),
            P("ctx", "tp"),
            P("ctx", "tp"),
            P("ctx", "tp"),
            P("ctx"),
            P("tp"),
            P("tp", None),
            P(None, None, "tp"),
        ),
        out_specs=(
            P("ctx", "tp"),
            P("ctx", "tp"),
            P("ctx", "tp"),
            P("tp"),
            P("tp", None),
            P(None, None, "tp"),
        ),
        check_vma=False,
    )
```

```python
import functools
import math

import jax
import jax.numpy as jnp
from jax import lax
from jax.experimental import pallas as pl
from jax.experimental.pallas import tpu as pltpu
from jax.sharding import PartitionSpec as P

F32 = jnp.float32
BF16 = jnp.bfloat16
MESH = pl.DeviceIdType.MESH
LANES = 128
HALF = 128
ROWS = 256
SHORT = 3
EPS = 1e-06
RING = 8


def iota(axis):
    return lax.broadcasted_iota(jnp.int32, (LANES, LANES), axis)


def as_column(row):
    eye = iota(0) == iota(1)
    spread = jnp.where(eye, jnp.broadcast_to(row, (LANES, LANES)), 0.0)
    return jnp.sum(spread, axis=1, keepdims=True)


def flip():
    return iota(0) + iota(1) == LANES - 1


def mirror():
    total = iota(0) + iota(1)
    return jnp.where((total == 0) | (total == LANES), 1.0, 0.0)


def kernel(
    ny,
    nz,
    ntp,
    q_hbm,
    k_hbm,
    v_hbm,
    go_hbm,
    docs_hbm,
    gain_hbm,
    filt_hbm,
    sw_hbm,
    gq_ref,
    gk_ref,
    gv_ref,
    gain_out,
    filt_out,
    short_out,
    docs_ref,
    gain_ref,
    filt_ref,
    sw_ref,
    xin,
    go_v,
    xf,
    feats,
    mixed,
    y_s,
    grads,
    prod,
    gmix,
    ring_f,
    ring_b,
    fmask,
    bmask,
    fmask32,
    filt32,
    filt_rev,
    wsc,
    dcol,
    m1,
    m2,
    docs_prev,
    docs_next,
    edge_f,
    edge_s,
    edge_r,
    tail_s,
    tail_r,
    tail_q_s,
    tail_q_r,
    acc,
    stats,
    scales,
    big,
    small,
    lhs_s,
    mirrored,
    red_e,
    red_l,
    e1,
    e2,
    fin_e,
    l1,
    l2,
    fin_l,
    load_sem,
    doc_sem,
    edge_sem,
    h1_send,
    h1_recv,
    h2_send,
    h2_recv,
    st_send,
    st_recv,
    tq_sem,
    e1_send,
    e1_recv,
    e2_send,
    e2_recv,
    e3_send,
    e3_recv,
    l1_send,
    l1_recv,
    l2_send,
    l2_recv,
    l3_send,
    l3_recv,
):
    nt = nz
    outs = (gq_ref, gk_ref, gv_ref)
    groups = filt_hbm.shape[0]
    per_tile = groups // nt
    width = LANES // per_tile
    n_ctx = ny * nz
    channels = nt * LANES
    total_channels = channels * ntp
    grad_scale = 1.0 / math.sqrt(ROWS * n_ctx)
    ctx = lax.axis_index("ctx")
    tp = lax.axis_index("tp")
    nxt = lax.rem(ctx + 1, n_ctx)
    prv = lax.rem(ctx + n_ctx - 1, n_ctx)
    y_at = lax.div(ctx, nz)
    z_at = lax.rem(ctx, nz)

    def z_peer(d):
        return lax.rem(z_at + d, nz)

    def y_peer(d):
        return lax.rem(y_at + d, ny)

    def tp_peer(d):
        return lax.rem(tp + d, ntp)

    def remote(src, dst, send, recv, where):
        return pltpu.make_async_remote_copy(
            src_ref=src, dst_ref=dst, send_sem=send, recv_sem=recv, device_id=where, device_id_type=MESH
        )

    loads = [
        pltpu.make_async_copy(k_hbm, xin.at[1], load_sem.at[1]),
        pltpu.make_async_copy(v_hbm, xin.at[2], load_sem.at[2]),
        pltpu.make_async_copy(q_hbm, xin.at[0], load_sem.at[0]),
        pltpu.make_async_copy(go_hbm, go_v, load_sem.at[3]),
    ]
    small_loads = [
        pltpu.make_async_copy(sw_hbm, sw_ref, load_sem.at[4]),
        pltpu.make_async_copy(docs_hbm, docs_ref, load_sem.at[5]),
        pltpu.make_async_copy(filt_hbm, filt_ref, load_sem.at[6]),
        pltpu.make_async_copy(gain_hbm, gain_ref, load_sem.at[7]),
    ]
    for load in small_loads + loads:
        load.start()

    barrier = pltpu.get_barrier_semaphore()
    partners = [(nxt, tp), (prv, tp)]
    partners += [(ctx, tp_peer(d)) for d in range(1, ntp)]
    partners += [(y_at * nz + z_peer(d), tp) for d in range(1, nz)]
    partners += [(y_peer(d) * nz + z_at, tp) for d in range(1, ny)]
    for where in partners:
        pl.semaphore_signal(barrier, inc=1, device_id=where, device_id_type=MESH)

    for load in small_loads:
        load.wait()
    for a in range(3):
        taps = sw_ref[a].astype(F32)
        for c in range(nt):
            wsc[c, a, 0:SHORT, :] = taps[:, c * LANES : (c + 1) * LANES]
    for c in range(nt):
        wsc[c, 3, 0:1, :] = gain_ref[c * LANES : (c + 1) * LANES].astype(F32).reshape(1, LANES)
    filt32[...] = filt_ref[...].astype(F32)
    filt_rev[...] = jnp.dot(filt_ref[...], mirror().astype(BF16), preferred_element_type=F32)

    docs_f = docs_ref[...].astype(F32)
    own = [docs_f[0:1], docs_f[1:2]]
    own_col = [as_column(row) for row in own]
    for n in range(2):
        dcol[8 + HALF * n : 8 + HALF * (n + 1), :] = jnp.broadcast_to(own_col[n], (HALF, LANES))

    def short_masks(start, size):
        here = dcol[8 + start : 8 + start + size, :]
        m1[start : start + size, :] = (dcol[7 + start : 7 + start + size, :] == here).astype(F32)
        m2[start : start + size, :] = (dcol[6 + start : 6 + start + size, :] == here).astype(F32)

    short_masks(HALF, HALF)

    for load in loads[:3]:
        load.wait()
    for a in range(3):
        last = xin[a, ROWS - 16 : ROWS, :].astype(F32)
        edge_f[2 * a : 2 * a + 2, :] = last[14:16]
    edge_f[6:8, :] = jnp.zeros((2, channels), F32)
    edge_s[...] = edge_f[...].astype(BF16)

    doc_fwd = remote(docs_ref, docs_prev, doc_sem.at[0], doc_sem.at[1], (nxt, tp))
    doc_bwd = remote(docs_ref, docs_next, doc_sem.at[2], doc_sem.at[3], (prv, tp))
    edge = remote(edge_s, edge_r, edge_sem.at[0], edge_sem.at[1], (nxt, tp))

    def cols(c):
        return pl.ds(pl.multiple_of(c * LANES, LANES), LANES)

    def feature(a, c, start):
        x0 = xf[a, c, pl.ds(8 + start, HALF), :]
        x1 = xf[a, c, pl.ds(7 + start, HALF), :]
        x2 = xf[a, c, pl.ds(6 + start, HALF), :]
        w = wsc[c, a]
        return (
            w[0:1] * x0
            + w[1:2] * x1 * m1[start : start + HALF, :]
            + w[2:3] * x2 * m2[start : start + HALF, :]
        )

    def halo1(c):
        return remote(
            prod.at[c, pl.ds(ROWS, HALF)], prod.at[c, pl.ds(0, HALF)], h1_send.at[c], h1_recv.at[c], (nxt, tp)
        )

    def halo2(c):
        return remote(
            gmix.at[c, pl.ds(0, HALF)], gmix.at[c, pl.ds(ROWS, HALF)], h2_send.at[c], h2_recv.at[c], (prv, tp)
        )

    def products(c, start):
        fk = feature(1, c, start)
        fv = feature(2, c, start)
        feats[1, c, start : start + HALF, :] = fk
        feats[2, c, start : start + HALF, :] = fv
        prod[c, HALF + start : 2 * HALF + start, :] = (fk * fv).astype(BF16)

    def late_half(c, carry):
        for a in (1, 2):
            xf[a, c, 8 : 8 + ROWS, :] = xin[a, :, cols(c)].astype(F32)
        products(c, HALF)
        halo1(c).start()
        return carry

    pl.semaphore_wait(barrier, len(partners))
    doc_fwd.start()
    doc_bwd.start()
    edge.start()
    lax.fori_loop(0, nt, late_half, 0)

    def build(source, target):
        def one(c, carry):
            rows = source[pl.ds(pl.multiple_of(c * per_tile, per_tile), per_tile), :]
            for g in range(per_tile):
                row = jnp.broadcast_to(rows[g : g + 1], (HALF, LANES))
                band = pltpu.roll(row, 0, 1, stride=1, stride_axis=0)
                target[c, g * HALF : (g + 1) * HALF, :] = band.astype(BF16)
            return carry

        lax.fori_loop(0, nt, one, 0)

    build(filt_rev, ring_f)
    build(filt32, ring_b)

    doc_fwd.wait_recv()
    doc_bwd.wait_recv()
    edge.wait_recv()
    row_prev = jnp.where(ctx == 0, -1.0, docs_prev[1:2, :].astype(F32))
    row_next = jnp.where(ctx == n_ctx - 1, -1.0, docs_next[0:1, :].astype(F32))
    col_prev = as_column(row_prev)
    col_next = as_column(row_next)
    dcol[0:8, :] = jnp.broadcast_to(col_prev[HALF - 8 :], (8, LANES))
    dcol[8 + ROWS : 16 + ROWS, :] = jnp.broadcast_to(col_next[:8], (8, LANES))
    short_masks(0, HALF)
    short_masks(ROWS, 8)
    i_at, j_at = iota(0), iota(1)

    def pick(keep, column, row):
        return jnp.where(keep & (column == row), 1.0, 0.0)

    flip_s = flip().astype(BF16)
    before_rows = (row_prev, own[0])
    after_rows = (own[1], row_next)
    for n in range(2):
        fmask[n, 0] = pick(j_at > i_at, own_col[n], before_rows[n]).astype(BF16)
        fmask[n, 1] = pick(j_at <= i_at, own_col[n], own[n]).astype(BF16)
        for side in range(2):
            fmask32[n, side] = jnp.dot(fmask[n, side], flip_s, preferred_element_type=F32)
        bmask[n, 0] = pick(j_at >= i_at, own_col[n], own[n]).astype(BF16)
        bmask[n, 1] = pick(j_at < i_at, own_col[n], after_rows[n]).astype(BF16)

    def early_half(c):
        xf[0, c, 8 : 8 + ROWS, :] = xin[0, :, cols(c)].astype(F32)
        came = edge_r[:, cols(c)].astype(F32)
        for a in range(3):
            xf[a, c, 6:8, :] = came[2 * a : 2 * a + 2]
        products(c, 0)
        for start in (0, HALF):
            feats[0, c, start : start + HALF, :] = feature(0, c, start)

    loads[3].wait()

    lane_group = lax.div(iota(1), width)

    def convolve(bands, masks, window, slot):
        for g in range(per_tile):
            rows = slice(g * HALF, (g + 1) * HALF)
            band = bands[rows, :]
            for side in range(2):
                lhs_s[slot, side, rows, :] = band * masks[side]
        lhs = jnp.concatenate([lhs_s[slot, 0], lhs_s[slot, 1]], axis=1)
        small[slot] = jnp.dot(lhs, window, preferred_element_type=F32)
        value = small[slot, 0:HALF, :]
        for g in range(1, per_tile):
            value = jnp.where(lane_group == g, small[slot, g * HALF : (g + 1) * HALF, :], value)
        return value

    def tiles(body, ready=None, unroll=2):
        def step(i, carry):
            if ready is not None:
                for u in range(unroll):
                    ready(i * unroll + u)
            for u in range(unroll):
                body(i * unroll + u, u)
            return carry

        lax.fori_loop(0, nt // unroll, step, 0)

    acc[...] = jnp.zeros_like(acc)

    def mirror_products(c, carry):
        for at in range(3):
            block = prod[c, at * HALF : (at + 1) * HALF, :]
            mirrored[c, at * HALF : (at + 1) * HALF, :] = jnp.dot(
                flip_s, block, preferred_element_type=F32
            ).astype(BF16)
        return carry

    def forward(n):
        span = slice(n * HALF, (n + 1) * HALF)

        def one(c, slot):
            if n == 1:
                early_half(c)
            value = convolve(ring_f.at[c], fmask[n], prod[c, n * HALF : n * HALF + ROWS, :], slot)
            mixed[c, span, :] = value
            y = feats[0, c, span, :] * value
            y_s[c, span, :] = y
            weighted = wsc[c, 3, 0:1, :] * go_v[span, cols(c)].astype(F32)
            acc[n, 0] += y * y
            acc[n, 1] += weighted * y

        tiles(one, (lambda c: halo1(c).wait_recv()) if n == 0 else None)

    forward(1)
    forward(0)

    stats[tp] = jnp.zeros((8, LANES), F32)
    for n in range(2):
        for kind in range(2):
            line = jnp.sum(acc[n, kind].T, axis=0, keepdims=True)
            stats[tp, 2 * kind + n : 2 * kind + n + 1, :] = line
    sends = [
        remote(stats.at[tp], stats.at[tp], st_send.at[d], st_recv.at[d], (ctx, tp_peer(d)))
        for d in range(1, ntp)
    ]
    for send in sends:
        send.start()
    lax.fori_loop(0, nt, mirror_products, 0)
    for d in range(1, ntp):
        came = stats.at[tp_peer(ntp - d)]
        remote(came, came, st_send.at[d], st_recv.at[d], (ctx, tp_peer(d))).wait_recv()
    sums = stats[0]
    for p in range(1, ntp):
        sums = sums + stats[p]
    scale = lax.rsqrt(sums[0:2] / total_channels + EPS)
    pull = scale * scale * scale * sums[2:4] / total_channels
    for n in range(2):
        scales[n, 0] = jnp.broadcast_to(as_column(scale[n : n + 1]), (HALF, LANES))
        scales[n, 1] = jnp.broadcast_to(as_column(pull[n : n + 1]), (HALF, LANES))

    def backward_norm(n):
        span = slice(n * HALF, (n + 1) * HALF)

        def one(c, carry=0):
            cot = go_v[span, cols(c)].astype(F32)
            y = y_s[c, span, :]
            row_scale = scales[n, 0]
            grad_y = row_scale * (wsc[c, 3, 0:1, :] * cot) - y * scales[n, 1]
            gain_part = jnp.sum(cot * y * row_scale, axis=0, keepdims=True)
            if n == 0:
                red_e[c, 8:9, :] = gain_part
            else:
                red_e[c, 8:9, :] += gain_part
            gmix[c, span, :] = (grad_y * feats[0, c, span, :]).astype(BF16)
            if n == 0:
                halo2(c).start()
            grads[0, c, span, :] = grad_y * mixed[c, span, :]
            if n == 0:
                tail_q_s[0:2, cols(c)] = grads[0, c, 0:2, :]
            return carry

        return one

    tail_q_s[2:8, :] = jnp.zeros((6, channels), F32)
    first_norm = backward_norm(0)
    lax.fori_loop(0, nt, first_norm, 0)
    tail_q = remote(tail_q_s, tail_q_r, tq_sem.at[0], tq_sem.at[1], (prv, tp))
    tail_q.start()
    last_norm = backward_norm(1)

    def tap_sums(a, c, grad, start):
        rows = slice(start, start + HALF)
        shifted = [xf[a, c, 8 - j + start : 8 - j + start + HALF, :] for j in range(SHORT)]
        terms = (grad * shifted[0], grad * m1[rows, :] * shifted[1], grad * m2[rows, :] * shifted[2])
        return [jnp.sum(term, axis=0, keepdims=True) for term in terms]

    def backward_conv(n):
        span = slice(n * HALF, (n + 1) * HALF)

        def one(c, slot):
            if n == 0:
                last_norm(c)
            value = convolve(ring_b.at[c], bmask[n], gmix[c, n * HALF : n * HALF + ROWS, :], slot)
            for a in (1, 2):
                grad = value * feats[3 - a, c, span, :]
                grads[a, c, span, :] = grad
                parts = tap_sums(a, c, grad, n * HALF)
                for j in range(SHORT):
                    at = slice(3 * a - 3 + j, 3 * a - 2 + j)
                    red_l[c, at, :] = parts[j] if n == 0 else red_l[c, at, :] + parts[j]
            if n == 0:
                tail_s[2:4, cols(c)] = grads[1, c, 0:2, :]
                tail_s[4:6, cols(c)] = grads[2, c, 0:2, :]
                red_l[c, 6:8, :] = jnp.zeros((2, LANES), F32)
                parts = [tap_sums(0, c, grads[0, c, s : s + HALF, :], s) for s in (0, HALF)]
                for j in range(SHORT):
                    red_e[c, 9 + j : 10 + j, :] = parts[0][j] + parts[1][j]

        tiles(one, (lambda c: halo2(c).wait_recv()) if n == 1 else None)

    tail_s[0:2, :] = jnp.zeros((2, channels), F32)
    tail_s[6:8, :] = jnp.zeros((2, channels), F32)
    backward_conv(0)
    tail = remote(tail_s, tail_r, edge_sem.at[2], edge_sem.at[3], (prv, tp))
    tail.start()

    def filter_sums(c, slot):
        for n in range(2):
            own_rows = gmix[c, n * HALF : (n + 1) * HALF, :]
            for g in range(per_tile):
                keep = (lane_group == g).astype(BF16)
                lhs_s[slot, n, g * HALF : (g + 1) * HALF, :] = own_rows * keep
            big[slot, n] = lax.dot_general(
                lhs_s[slot, n],
                mirrored[c, n * HALF : n * HALF + ROWS, :],
                (((1,), (1,)), ((), ())),
                preferred_element_type=F32,
            )
        for g in range(per_tile):
            rows = slice(g * HALF, (g + 1) * HALF)
            folded = jnp.zeros((HALF, LANES), F32)
            for n in range(2):
                folded += big[slot, n, rows, 0:LANES] * fmask32[n, 0]
                folded += big[slot, n, rows, LANES:] * fmask32[n, 1]
            turned = pltpu.roll(folded, 1, 1, stride=1, stride_axis=0)
            red_e[c, g : g + 1, :] = jnp.sum(turned, axis=0, keepdims=True)
        red_e[c, 12:16, :] = jnp.zeros((4, LANES), F32)

    def write_grads(c, carry):
        for a, came in enumerate((tail_q_r, tail_r, tail_r)):
            grads[a, c, ROWS : ROWS + 2, :] = came[2 * a : 2 * a + 2, cols(c)]
            w = wsc[c, a]
            for start in (0, HALF):
                h0, h1, h2 = [grads[a, c, start + j : start + j + HALF, :] for j in range(SHORT)]
                h1 = h1 * m1[start + 1 : start + 1 + HALF, :]
                h2 = h2 * m2[start + 2 : start + 2 + HALF, :]
                value = w[0:1] * h0 + w[1:2] * h1 + w[2:3] * h2
                outs[a][start : start + HALF, cols(c)] = value.astype(BF16)
        return carry

    share = nt // ny

    def tiles_of(at):
        return pl.ds(at * share, share)

    def to_owners(own, came, send, recv):
        return [
            remote(own.at[tiles_of(y_peer(d))], came.at[d], send.at[d], recv.at[d], (y_peer(d) * nz + z_at, tp))
            for d in range(1, ny)
        ]

    def to_z(came, send, recv):
        return [
            remote(came.at[z_at], came.at[z_at], send.at[d], recv.at[d], (y_at * nz + z_peer(d), tp))
            for d in range(1, nz)
        ]

    def to_y(whole, send, recv):
        mine = whole.at[tiles_of(y_at)]
        return [remote(mine, mine, send.at[d], recv.at[d], (y_peer(d) * nz + z_at, tp)) for d in range(1, ny)]

    def launch(copies):
        for copy in copies:
            copy.start()

    def add_owned(own, came, copies, target):
        part = own[tiles_of(y_at)]
        for d in range(1, ny):
            copies[d - 1].wait_recv()
            part = part + came[d]
        target[z_at] = part

    def add_z(came, send, recv, whole):
        for d in range(1, nz):
            slot = came.at[z_peer(nz - d)]
            remote(slot, slot, send.at[d], recv.at[d], (y_at * nz + z_peer(d), tp)).wait_recv()
        part = came[0]
        for p in range(1, nz):
            part = part + came[p]
        whole[tiles_of(y_at)] = part * grad_scale

    def wait_y(whole, send, recv):
        for d in range(1, ny):
            slot = whole.at[tiles_of(y_peer(ny - d))]
            remote(slot, slot, send.at[d], recv.at[d], (y_peer(d) * nz + z_at, tp)).wait_recv()

    tiles(filter_sums)
    e_owner = to_owners(red_e, e1, e1_send, e1_recv)
    launch(e_owner)
    backward_conv(1)
    l_owner = to_owners(red_l, l1, l1_send, l1_recv)
    launch(l_owner)
    add_owned(red_e, e1, e_owner, e2)
    e_z = to_z(e2, e2_send, e2_recv)
    launch(e_z)
    tail_q.wait_recv()
    tail.wait_recv()
    lax.fori_loop(0, nt, write_grads, 0)
    add_owned(red_l, l1, l_owner, l2)
    l_z = to_z(l2, l2_send, l2_recv)
    launch(l_z)
    add_z(e2, e2_send, e2_recv, fin_e)
    e_y = to_y(fin_e, e3_send, e3_recv)
    launch(e_y)
    add_z(l2, l2_send, l2_recv, fin_l)
    l_y = to_y(fin_l, l3_send, l3_recv)
    launch(l_y)
    wait_y(fin_e, e3_send, e3_recv)
    for c in range(nt):
        span = slice(c * LANES, (c + 1) * LANES)
        filt_out[c * per_tile : (c + 1) * per_tile, :] = fin_e[c, 0:per_tile, :]
        gain_out[:, span] = fin_e[c, 8:9, :]
        short_out[0, :, span] = fin_e[c, 9:12, :]
    wait_y(fin_l, l3_send, l3_recv)
    for c in range(nt):
        span = slice(c * LANES, (c + 1) * LANES)
        for a in (1, 2):
            short_out[a, :, span] = fin_l[c, 3 * a - 3 : 3 * a, :]

    for copy in [doc_fwd, doc_bwd, edge, tail_q, tail] + sends + e_owner + e_z + e_y + l_owner + l_z + l_y:
        copy.wait_send()

    def drain(c, carry):
        halo1(c).wait_send()
        halo2(c).wait_send()
        return carry

    lax.fori_loop(0, nt, drain, 0)


def resident(shape, dtype):
    return pltpu.VMEM(shape, dtype)


def pinned(value):
    return pltpu.with_memory_space_constraint(value, pltpu.VMEM)


def publish(*refs):
    count = (len(refs) - 1) // 2
    sem = refs[-1]
    copies = [pltpu.make_async_copy(refs[i], refs[count + i], sem.at[i]) for i in range(count)]
    for copy in copies:
        copy.start()
    for copy in copies:
        copy.wait()


def on_device(nz, q_in, k_in, v_in, grad_out, doc_ids, gain, filters, short_weight):
    rows, channels = q_in.shape
    groups, taps = filters.shape
    ntp = lax.axis_size("tp")
    ny = lax.axis_size("ctx") // nz
    nt = channels // LANES
    assert rows == ROWS and taps == HALF and nt == nz and groups == 8 * nt
    hbm = pl.BlockSpec(memory_space=pl.ANY)
    vmem = pl.BlockSpec(memory_space=pltpu.VMEM)
    tall = resident((rows, channels), BF16)
    dma = pltpu.SemaphoreType.DMA
    held = pl.pallas_call(
        functools.partial(kernel, ny, nz, ntp),
        name="mixer_backward",
        out_shape=(
            tall,
            tall,
            tall,
            resident((1, channels), F32),
            resident((groups, taps), F32),
            resident((3, SHORT, channels), F32),
        ),
        in_specs=[pl.BlockSpec(memory_space=pltpu.HBM)] * 8,
        out_specs=(vmem,) * 6,
        scratch_shapes=[
            pltpu.VMEM((2, LANES), jnp.int32),
            pltpu.VMEM((channels,), BF16),
            pltpu.VMEM((groups, taps), BF16),
            pltpu.VMEM((3, SHORT, channels), BF16),
            pltpu.VMEM((3, rows, channels), BF16),
            pltpu.VMEM((rows, channels), BF16),
            pltpu.VMEM((3, nt, rows + 8, LANES), F32),
            pltpu.VMEM((3, nt, rows, LANES), F32),
            pltpu.VMEM((nt, rows, LANES), F32),
            pltpu.VMEM((nt, rows, LANES), F32),
            pltpu.VMEM((3, nt, rows + 8, LANES), F32),
            pltpu.VMEM((nt, rows + HALF, LANES), BF16),
            pltpu.VMEM((nt, rows + HALF, LANES), BF16),
            pltpu.VMEM((nt, 8 * HALF, LANES), BF16),
            pltpu.VMEM((nt, 8 * HALF, LANES), BF16),
            pltpu.VMEM((2, 2, HALF, LANES), BF16),
            pltpu.VMEM((2, 2, HALF, LANES), BF16),
            pltpu.VMEM((2, 2, HALF, LANES), F32),
            pltpu.VMEM((groups, LANES), F32),
            pltpu.VMEM((groups, LANES), F32),
            pltpu.VMEM((nt, 4, 8, LANES), F32),
            pltpu.VMEM((rows + 16, LANES), F32),
            pltpu.VMEM((rows + 8, LANES), F32),
            pltpu.VMEM((rows + 8, LANES), F32),
            pltpu.VMEM((2, LANES), jnp.int32),
            pltpu.VMEM((2, LANES), jnp.int32),
            pltpu.VMEM((8, channels), F32),
            pltpu.VMEM((8, channels), BF16),
            pltpu.VMEM((8, channels), BF16),
            pltpu.VMEM((8, channels), F32),
            pltpu.VMEM((8, channels), F32),
            pltpu.VMEM((8, channels), F32),
            pltpu.VMEM((8, channels), F32),
            pltpu.VMEM((2, 2, HALF, LANES), F32),
            pltpu.VMEM((ntp, 8, LANES), F32),
            pltpu.VMEM((2, 2, HALF, LANES), F32),
            pltpu.VMEM((2, 2, 8 * HALF, 2 * LANES), F32),
            pltpu.VMEM((2, 8 * HALF, LANES), F32),
            pltpu.VMEM((2, 2, 8 * HALF, LANES), BF16),
            pltpu.VMEM((nt, rows + HALF, LANES), BF16),
            pltpu.VMEM((nt, 16, LANES), F32),
            pltpu.VMEM((nt, 8, LANES), F32),
            pltpu.VMEM((ny, nt // ny, 16, LANES), F32),
            pltpu.VMEM((nz, nt // ny, 16, LANES), F32),
            pltpu.VMEM((nt, 16, LANES), F32),
            pltpu.VMEM((ny, nt // ny, 8, LANES), F32),
            pltpu.VMEM((nz, nt // ny, 8, LANES), F32),
            pltpu.VMEM((nt, 8, LANES), F32),
            dma((8,)),
            dma((4,)),
            dma((4,)),
            dma((nt,)),
            dma((nt,)),
            dma((nt,)),
            dma((nt,)),
            dma((ntp,)),
            dma((ntp,)),
            dma((2,)),
            dma((ny,)),
            dma((ny,)),
            dma((nz,)),
            dma((nz,)),
            dma((ny,)),
            dma((ny,)),
            dma((ny,)),
            dma((ny,)),
            dma((nz,)),
            dma((nz,)),
            dma((ny,)),
            dma((ny,)),
        ],
        compiler_params=pltpu.CompilerParams(
            collective_id=0, has_side_effects=True, vmem_limit_bytes=60 * 1024 * 1024
        ),
    )(
        q_in,
        k_in,
        v_in,
        grad_out,
        doc_ids.reshape(2, LANES),
        gain,
        filters,
        short_weight,
    )
    out = pl.pallas_call(
        publish,
        name="publish",
        out_shape=[jax.ShapeDtypeStruct(x.shape, x.dtype) for x in held],
        in_specs=[vmem] * 6,
        out_specs=[hbm] * 6,
        scratch_shapes=[dma((6,))],
    )(*[pinned(x) for x in held])
    return out[0], out[1], out[2], out[3].reshape(channels), out[4], out[5]


def solution(mesh, ring=RING):
    return jax.shard_map(
        functools.partial(on_device, ring),
        mesh=mesh,
        in_specs=(
            P("ctx", "tp"),
            P("ctx", "tp"),
            P("ctx", "tp"),
            P("ctx", "tp"),
            P("ctx"),
            P("tp"),
            P("tp", None),
            P(None, None, "tp"),
        ),
        out_specs=(
            P("ctx", "tp"),
            P("ctx", "tp"),
            P("ctx", "tp"),
            P("tp"),
            P("tp", None),
            P(None, None, "tp"),
        ),
        check_vma=False,
    )
```

```python
import functools
import math

import jax
import jax.numpy as jnp
from jax import lax
from jax.experimental import pallas as pl
from jax.experimental.pallas import tpu as pltpu
from jax.sharding import PartitionSpec as P

F32 = jnp.float32
BF16 = jnp.bfloat16
MESH = pl.DeviceIdType.MESH
LANES = 128
HALF = 128
ROWS = 256
SHORT = 3
EPS = 1e-06
RING = 8


def iota(axis):
    return lax.broadcasted_iota(jnp.int32, (LANES, LANES), axis)


def as_column(row):
    eye = iota(0) == iota(1)
    spread = jnp.where(eye, jnp.broadcast_to(row, (LANES, LANES)), 0.0)
    return jnp.sum(spread, axis=1, keepdims=True)


def flip():
    return iota(0) + iota(1) == LANES - 1


def far_first(count):
    return sorted(range(1, count), key=lambda d: abs(2 * d - count))


def mirror():
    total = iota(0) + iota(1)
    return jnp.where((total == 0) | (total == LANES), 1.0, 0.0)


def kernel(
    ny,
    nz,
    ntp,
    q_hbm,
    k_hbm,
    v_hbm,
    go_hbm,
    docs_hbm,
    gain_hbm,
    filt_hbm,
    sw_hbm,
    gq_ref,
    gk_ref,
    gv_ref,
    gain_out,
    filt_out,
    short_out,
    docs_ref,
    gain_ref,
    filt_ref,
    sw_ref,
    xin,
    go_v,
    xf,
    feats,
    mixed,
    y_s,
    grads,
    prod,
    gmix,
    ring_f,
    ring_b,
    fmask,
    bmask,
    fmask32,
    filt32,
    filt_rev,
    wsc,
    dcol,
    m1,
    m2,
    docs_prev,
    docs_next,
    edge_f,
    edge_s,
    edge_r,
    tail_s,
    tail_r,
    tail_q_s,
    tail_q_r,
    acc,
    stats,
    scales,
    big,
    small,
    lhs_s,
    mirrored,
    red_e,
    red_l,
    e1,
    e2,
    fin_e,
    l1,
    l2,
    fin_l,
    load_sem,
    doc_sem,
    edge_sem,
    h1_send,
    h1_recv,
    h2_send,
    h2_recv,
    st_send,
    st_recv,
    tq_sem,
    e1_send,
    e1_recv,
    e2_send,
    e2_recv,
    e3_send,
    e3_recv,
    l1_send,
    l1_recv,
    l2_send,
    l2_recv,
    l3_send,
    l3_recv,
):
    nt = nz
    outs = (gq_ref, gk_ref, gv_ref)
    groups = filt_hbm.shape[0]
    per_tile = groups // nt
    width = LANES // per_tile
    n_ctx = ny * nz
    channels = nt * LANES
    total_channels = channels * ntp
    grad_scale = 1.0 / math.sqrt(ROWS * n_ctx)
    ctx = lax.axis_index("ctx")
    tp = lax.axis_index("tp")
    nxt = lax.rem(ctx + 1, n_ctx)
    prv = lax.rem(ctx + n_ctx - 1, n_ctx)
    y_at = lax.div(ctx, nz)
    z_at = lax.rem(ctx, nz)

    def z_peer(d):
        return lax.rem(z_at + d, nz)

    def y_peer(d):
        return lax.rem(y_at + d, ny)

    def tp_peer(d):
        return lax.rem(tp + d, ntp)

    def remote(src, dst, send, recv, where):
        return pltpu.make_async_remote_copy(
            src_ref=src, dst_ref=dst, send_sem=send, recv_sem=recv, device_id=where, device_id_type=MESH
        )

    loads = [
        pltpu.make_async_copy(k_hbm, xin.at[1], load_sem.at[1]),
        pltpu.make_async_copy(v_hbm, xin.at[2], load_sem.at[2]),
        pltpu.make_async_copy(q_hbm, xin.at[0], load_sem.at[0]),
        pltpu.make_async_copy(go_hbm, go_v, load_sem.at[3]),
    ]
    small_loads = [
        pltpu.make_async_copy(sw_hbm, sw_ref, load_sem.at[4]),
        pltpu.make_async_copy(docs_hbm, docs_ref, load_sem.at[5]),
        pltpu.make_async_copy(filt_hbm, filt_ref, load_sem.at[6]),
        pltpu.make_async_copy(gain_hbm, gain_ref, load_sem.at[7]),
    ]
    for load in small_loads + loads:
        load.start()

    barrier = pltpu.get_barrier_semaphore()
    partners = [(nxt, tp), (prv, tp)]
    partners += [(ctx, tp_peer(d)) for d in range(1, ntp)]
    partners += [(y_at * nz + z_peer(d), tp) for d in range(1, nz)]
    partners += [(y_peer(d) * nz + z_at, tp) for d in range(1, ny)]
    for where in partners:
        pl.semaphore_signal(barrier, inc=1, device_id=where, device_id_type=MESH)

    for load in small_loads:
        load.wait()
    for a in range(3):
        taps = sw_ref[a].astype(F32)
        for c in range(nt):
            wsc[c, a, 0:SHORT, :] = taps[:, c * LANES : (c + 1) * LANES]
    for c in range(nt):
        wsc[c, 3, 0:1, :] = gain_ref[c * LANES : (c + 1) * LANES].astype(F32).reshape(1, LANES)
    filt32[...] = filt_ref[...].astype(F32)
    filt_rev[...] = jnp.dot(filt_ref[...], mirror().astype(BF16), preferred_element_type=F32)

    docs_f = docs_ref[...].astype(F32)
    own = [docs_f[0:1], docs_f[1:2]]
    own_col = [as_column(row) for row in own]
    for n in range(2):
        dcol[8 + HALF * n : 8 + HALF * (n + 1), :] = jnp.broadcast_to(own_col[n], (HALF, LANES))

    def short_masks(start, size):
        here = dcol[8 + start : 8 + start + size, :]
        m1[start : start + size, :] = (dcol[7 + start : 7 + start + size, :] == here).astype(F32)
        m2[start : start + size, :] = (dcol[6 + start : 6 + start + size, :] == here).astype(F32)

    short_masks(HALF, HALF)

    for load in loads[:3]:
        load.wait()
    for a in range(3):
        last = xin[a, ROWS - 16 : ROWS, :].astype(F32)
        edge_f[2 * a : 2 * a + 2, :] = last[14:16]
    edge_f[6:8, :] = jnp.zeros((2, channels), F32)
    edge_s[...] = edge_f[...].astype(BF16)

    doc_fwd = remote(docs_ref, docs_prev, doc_sem.at[0], doc_sem.at[1], (nxt, tp))
    doc_bwd = remote(docs_ref, docs_next, doc_sem.at[2], doc_sem.at[3], (prv, tp))
    edge = remote(edge_s, edge_r, edge_sem.at[0], edge_sem.at[1], (nxt, tp))

    def cols(c):
        return pl.ds(pl.multiple_of(c * LANES, LANES), LANES)

    def feature(a, c, start):
        x0 = xf[a, c, pl.ds(8 + start, HALF), :]
        x1 = xf[a, c, pl.ds(7 + start, HALF), :]
        x2 = xf[a, c, pl.ds(6 + start, HALF), :]
        w = wsc[c, a]
        return (
            w[0:1] * x0
            + w[1:2] * x1 * m1[start : start + HALF, :]
            + w[2:3] * x2 * m2[start : start + HALF, :]
        )

    def halo1(c):
        return remote(
            prod.at[c, pl.ds(ROWS, HALF)], prod.at[c, pl.ds(0, HALF)], h1_send.at[c], h1_recv.at[c], (nxt, tp)
        )

    def halo2(c):
        return remote(
            gmix.at[c, pl.ds(0, HALF)], gmix.at[c, pl.ds(ROWS, HALF)], h2_send.at[c], h2_recv.at[c], (prv, tp)
        )

    def products(c, start):
        fk = feature(1, c, start)
        fv = feature(2, c, start)
        feats[1, c, start : start + HALF, :] = fk
        feats[2, c, start : start + HALF, :] = fv
        prod[c, HALF + start : 2 * HALF + start, :] = (fk * fv).astype(BF16)

    def late_half(c, carry):
        for a in (1, 2):
            xf[a, c, 8 : 8 + ROWS, :] = xin[a, :, cols(c)].astype(F32)
        products(c, HALF)
        halo1(c).start()
        return carry

    pl.semaphore_wait(barrier, len(partners))
    doc_fwd.start()
    doc_bwd.start()
    edge.start()
    lax.fori_loop(0, nt, late_half, 0)

    def build(source, target):
        def one(c, carry):
            rows = source[pl.ds(pl.multiple_of(c * per_tile, per_tile), per_tile), :]
            for g in range(per_tile):
                row = jnp.broadcast_to(rows[g : g + 1], (HALF, LANES))
                band = pltpu.roll(row, 0, 1, stride=1, stride_axis=0)
                target[c, g * HALF : (g + 1) * HALF, :] = band.astype(BF16)
            return carry

        lax.fori_loop(0, nt, one, 0)

    build(filt_rev, ring_f)

    doc_fwd.wait_recv()
    doc_bwd.wait_recv()
    edge.wait_recv()
    row_prev = jnp.where(ctx == 0, -1.0, docs_prev[1:2, :].astype(F32))
    row_next = jnp.where(ctx == n_ctx - 1, -1.0, docs_next[0:1, :].astype(F32))
    col_prev = as_column(row_prev)
    col_next = as_column(row_next)
    dcol[0:8, :] = jnp.broadcast_to(col_prev[HALF - 8 :], (8, LANES))
    dcol[8 + ROWS : 16 + ROWS, :] = jnp.broadcast_to(col_next[:8], (8, LANES))
    short_masks(0, HALF)
    short_masks(ROWS, 8)
    i_at, j_at = iota(0), iota(1)

    def pick(keep, column, row):
        return jnp.where(keep & (column == row), 1.0, 0.0)

    flip_s = flip().astype(BF16)
    before_rows = (row_prev, own[0])
    after_rows = (own[1], row_next)
    for n in range(2):
        fmask[n, 0] = pick(j_at > i_at, own_col[n], before_rows[n]).astype(BF16)
        fmask[n, 1] = pick(j_at <= i_at, own_col[n], own[n]).astype(BF16)
        for side in range(2):
            fmask32[n, side] = jnp.dot(fmask[n, side], flip_s, preferred_element_type=F32)
        bmask[n, 0] = pick(j_at >= i_at, own_col[n], own[n]).astype(BF16)
        bmask[n, 1] = pick(j_at < i_at, own_col[n], after_rows[n]).astype(BF16)

    def early_half(c):
        xf[0, c, 8 : 8 + ROWS, :] = xin[0, :, cols(c)].astype(F32)
        came = edge_r[:, cols(c)].astype(F32)
        for a in range(3):
            xf[a, c, 6:8, :] = came[2 * a : 2 * a + 2]
        products(c, 0)
        for start in (0, HALF):
            feats[0, c, start : start + HALF, :] = feature(0, c, start)

    loads[3].wait()

    lane_group = lax.div(iota(1), width)

    def convolve(bands, masks, window, slot):
        for g in range(per_tile):
            rows = slice(g * HALF, (g + 1) * HALF)
            band = bands[rows, :]
            for side in range(2):
                lhs_s[slot, side, rows, :] = band * masks[side]
        lhs = jnp.concatenate([lhs_s[slot, 0], lhs_s[slot, 1]], axis=1)
        small[slot] = jnp.dot(lhs, window, preferred_element_type=F32)
        value = small[slot, 0:HALF, :]
        for g in range(1, per_tile):
            value = jnp.where(lane_group == g, small[slot, g * HALF : (g + 1) * HALF, :], value)
        return value

    def tiles(body, ready=None, unroll=2):
        def step(i, carry):
            if ready is not None:
                for u in range(unroll):
                    ready(i * unroll + u)
            for u in range(unroll):
                body(i * unroll + u, u)
            return carry

        lax.fori_loop(0, nt // unroll, step, 0)

    acc[...] = jnp.zeros_like(acc)

    def mirror_products(c, carry):
        for at in range(3):
            block = prod[c, at * HALF : (at + 1) * HALF, :]
            mirrored[c, at * HALF : (at + 1) * HALF, :] = jnp.dot(
                flip_s, block, preferred_element_type=F32
            ).astype(BF16)
        return carry

    def forward(n):
        span = slice(n * HALF, (n + 1) * HALF)

        def one(c, slot):
            if n == 1:
                early_half(c)
            value = convolve(ring_f.at[c], fmask[n], prod[c, n * HALF : n * HALF + ROWS, :], slot)
            mixed[c, span, :] = value
            y = feats[0, c, span, :] * value
            y_s[c, span, :] = y
            weighted = wsc[c, 3, 0:1, :] * go_v[span, cols(c)].astype(F32)
            acc[n, 0] += y * y
            acc[n, 1] += weighted * y

        tiles(one, (lambda c: halo1(c).wait_recv()) if n == 0 else None)

    forward(1)
    forward(0)

    stats[tp] = jnp.zeros((8, LANES), F32)
    for n in range(2):
        for kind in range(2):
            line = jnp.sum(acc[n, kind].T, axis=0, keepdims=True)
            stats[tp, 2 * kind + n : 2 * kind + n + 1, :] = line
    sends = [
        remote(stats.at[tp], stats.at[tp], st_send.at[d], st_recv.at[d], (ctx, tp_peer(d)))
        for d in range(1, ntp)
    ]
    for d in far_first(ntp):
        sends[d - 1].start()
    build(filt32, ring_b)
    lax.fori_loop(0, nt, mirror_products, 0)
    for d in range(1, ntp):
        came = stats.at[tp_peer(ntp - d)]
        remote(came, came, st_send.at[d], st_recv.at[d], (ctx, tp_peer(d))).wait_recv()
    sums = stats[0]
    for p in range(1, ntp):
        sums = sums + stats[p]
    scale = lax.rsqrt(sums[0:2] / total_channels + EPS)
    pull = scale * scale * scale * sums[2:4] / total_channels
    for n in range(2):
        scales[n, 0] = jnp.broadcast_to(as_column(scale[n : n + 1]), (HALF, LANES))
        scales[n, 1] = jnp.broadcast_to(as_column(pull[n : n + 1]), (HALF, LANES))

    def backward_norm(n):
        span = slice(n * HALF, (n + 1) * HALF)

        def one(c, carry=0):
            cot = go_v[span, cols(c)].astype(F32)
            y = y_s[c, span, :]
            row_scale = scales[n, 0]
            grad_y = row_scale * (wsc[c, 3, 0:1, :] * cot) - y * scales[n, 1]
            gain_part = jnp.sum(cot * y * row_scale, axis=0, keepdims=True)
            if n == 0:
                red_e[c, 8:9, :] = gain_part
            else:
                red_e[c, 8:9, :] += gain_part
            gmix[c, span, :] = (grad_y * feats[0, c, span, :]).astype(BF16)
            if n == 0:
                halo2(c).start()
            grads[0, c, span, :] = grad_y * mixed[c, span, :]
            if n == 0:
                tail_q_s[0:2, cols(c)] = grads[0, c, 0:2, :]
            return carry

        return one

    tail_q_s[2:8, :] = jnp.zeros((6, channels), F32)
    first_norm = backward_norm(0)
    lax.fori_loop(0, nt, first_norm, 0)
    tail_q = remote(tail_q_s, tail_q_r, tq_sem.at[0], tq_sem.at[1], (prv, tp))
    tail_q.start()
    last_norm = backward_norm(1)

    def tap_sums(a, c, grad, start):
        rows = slice(start, start + HALF)
        shifted = [xf[a, c, 8 - j + start : 8 - j + start + HALF, :] for j in range(SHORT)]
        terms = (grad * shifted[0], grad * m1[rows, :] * shifted[1], grad * m2[rows, :] * shifted[2])
        return [jnp.sum(term, axis=0, keepdims=True) for term in terms]

    def backward_conv(n):
        span = slice(n * HALF, (n + 1) * HALF)

        def one(c, slot):
            if n == 0:
                last_norm(c)
            value = convolve(ring_b.at[c], bmask[n], gmix[c, n * HALF : n * HALF + ROWS, :], slot)
            for a in (1, 2):
                grad = value * feats[3 - a, c, span, :]
                grads[a, c, span, :] = grad
                parts = tap_sums(a, c, grad, n * HALF)
                for j in range(SHORT):
                    at = slice(3 * a - 3 + j, 3 * a - 2 + j)
                    red_l[c, at, :] = parts[j] if n == 0 else red_l[c, at, :] + parts[j]
            if n == 0:
                tail_s[2:4, cols(c)] = grads[1, c, 0:2, :]
                tail_s[4:6, cols(c)] = grads[2, c, 0:2, :]
                red_l[c, 6:8, :] = jnp.zeros((2, LANES), F32)
                parts = [tap_sums(0, c, grads[0, c, s : s + HALF, :], s) for s in (0, HALF)]
                for j in range(SHORT):
                    red_e[c, 9 + j : 10 + j, :] = parts[0][j] + parts[1][j]

        tiles(one, (lambda c: halo2(c).wait_recv()) if n == 1 else None)

    tail_s[0:2, :] = jnp.zeros((2, channels), F32)
    tail_s[6:8, :] = jnp.zeros((2, channels), F32)
    backward_conv(0)
    tail = remote(tail_s, tail_r, edge_sem.at[2], edge_sem.at[3], (prv, tp))
    tail.start()

    def filter_sums(c, slot):
        for n in range(2):
            own_rows = gmix[c, n * HALF : (n + 1) * HALF, :]
            for g in range(per_tile):
                keep = (lane_group == g).astype(BF16)
                lhs_s[slot, n, g * HALF : (g + 1) * HALF, :] = own_rows * keep
            big[slot, n] = lax.dot_general(
                lhs_s[slot, n],
                mirrored[c, n * HALF : n * HALF + ROWS, :],
                (((1,), (1,)), ((), ())),
                preferred_element_type=F32,
            )
        for g in range(per_tile):
            rows = slice(g * HALF, (g + 1) * HALF)
            folded = jnp.zeros((HALF, LANES), F32)
            for n in range(2):
                folded += big[slot, n, rows, 0:LANES] * fmask32[n, 0]
                folded += big[slot, n, rows, LANES:] * fmask32[n, 1]
            turned = pltpu.roll(folded, 1, 1, stride=1, stride_axis=0)
            red_e[c, g : g + 1, :] = jnp.sum(turned, axis=0, keepdims=True)
        red_e[c, 12:16, :] = jnp.zeros((4, LANES), F32)

    def write_grads(c, carry):
        for a, came in enumerate((tail_q_r, tail_r, tail_r)):
            grads[a, c, ROWS : ROWS + 2, :] = came[2 * a : 2 * a + 2, cols(c)]
            w = wsc[c, a]
            for start in (0, HALF):
                h0, h1, h2 = [grads[a, c, start + j : start + j + HALF, :] for j in range(SHORT)]
                h1 = h1 * m1[start + 1 : start + 1 + HALF, :]
                h2 = h2 * m2[start + 2 : start + 2 + HALF, :]
                value = w[0:1] * h0 + w[1:2] * h1 + w[2:3] * h2
                outs[a][start : start + HALF, cols(c)] = value.astype(BF16)
        return carry

    share = nt // ny

    def tiles_of(at):
        return pl.ds(at * share, share)

    def to_owners(own, came, send, recv):
        return [
            remote(own.at[tiles_of(y_peer(d))], came.at[d], send.at[d], recv.at[d], (y_peer(d) * nz + z_at, tp))
            for d in range(1, ny)
        ]

    def to_z(came, send, recv):
        return [
            remote(came.at[z_at], came.at[z_at], send.at[d], recv.at[d], (y_at * nz + z_peer(d), tp))
            for d in range(1, nz)
        ]

    def to_y(whole, send, recv):
        mine = whole.at[tiles_of(y_at)]
        return [remote(mine, mine, send.at[d], recv.at[d], (y_peer(d) * nz + z_at, tp)) for d in range(1, ny)]

    def launch(copies):
        for d in far_first(len(copies) + 1):
            copies[d - 1].start()

    def add_owned(own, came, copies, target):
        part = own[tiles_of(y_at)]
        for d in range(1, ny):
            copies[d - 1].wait_recv()
            part = part + came[d]
        target[z_at] = part

    def add_z(came, send, recv, whole):
        for d in range(1, nz):
            slot = came.at[z_peer(nz - d)]
            remote(slot, slot, send.at[d], recv.at[d], (y_at * nz + z_peer(d), tp)).wait_recv()
        part = came[0]
        for p in range(1, nz):
            part = part + came[p]
        whole[tiles_of(y_at)] = part * grad_scale

    def wait_y(whole, send, recv):
        for d in range(1, ny):
            slot = whole.at[tiles_of(y_peer(ny - d))]
            remote(slot, slot, send.at[d], recv.at[d], (y_peer(d) * nz + z_at, tp)).wait_recv()

    tiles(filter_sums)
    e_owner = to_owners(red_e, e1, e1_send, e1_recv)
    launch(e_owner)
    backward_conv(1)
    l_owner = to_owners(red_l, l1, l1_send, l1_recv)
    launch(l_owner)
    add_owned(red_e, e1, e_owner, e2)
    e_z = to_z(e2, e2_send, e2_recv)
    launch(e_z)
    tail_q.wait_recv()
    tail.wait_recv()
    lax.fori_loop(0, nt, write_grads, 0)
    add_owned(red_l, l1, l_owner, l2)
    l_z = to_z(l2, l2_send, l2_recv)
    launch(l_z)
    add_z(e2, e2_send, e2_recv, fin_e)
    e_y = to_y(fin_e, e3_send, e3_recv)
    launch(e_y)
    add_z(l2, l2_send, l2_recv, fin_l)
    l_y = to_y(fin_l, l3_send, l3_recv)
    launch(l_y)
    wait_y(fin_e, e3_send, e3_recv)
    for c in range(nt):
        span = slice(c * LANES, (c + 1) * LANES)
        filt_out[c * per_tile : (c + 1) * per_tile, :] = fin_e[c, 0:per_tile, :]
        gain_out[:, span] = fin_e[c, 8:9, :]
        short_out[0, :, span] = fin_e[c, 9:12, :]
    for copy in [doc_fwd, doc_bwd, edge, tail_q, tail] + sends + e_owner + e_z + e_y + l_owner + l_z:
        copy.wait_send()

    def drain(c, carry):
        halo1(c).wait_send()
        halo2(c).wait_send()
        return carry

    lax.fori_loop(0, nt, drain, 0)
    wait_y(fin_l, l3_send, l3_recv)
    for c in range(nt):
        span = slice(c * LANES, (c + 1) * LANES)
        for a in (1, 2):
            short_out[a, :, span] = fin_l[c, 3 * a - 3 : 3 * a, :]

    for copy in l_y:
        copy.wait_send()


def resident(shape, dtype):
    return pltpu.VMEM(shape, dtype)


def pinned(value):
    return pltpu.with_memory_space_constraint(value, pltpu.VMEM)


def publish(*refs):
    count = (len(refs) - 1) // 2
    sem = refs[-1]
    copies = [pltpu.make_async_copy(refs[i], refs[count + i], sem.at[i]) for i in range(count)]
    for copy in copies:
        copy.start()
    for copy in copies:
        copy.wait()


def on_device(nz, q_in, k_in, v_in, grad_out, doc_ids, gain, filters, short_weight):
    rows, channels = q_in.shape
    groups, taps = filters.shape
    ntp = lax.axis_size("tp")
    ny = lax.axis_size("ctx") // nz
    nt = channels // LANES
    assert rows == ROWS and taps == HALF and nt == nz and groups == 8 * nt
    hbm = pl.BlockSpec(memory_space=pl.ANY)
    vmem = pl.BlockSpec(memory_space=pltpu.VMEM)
    tall = resident((rows, channels), BF16)
    dma = pltpu.SemaphoreType.DMA
    held = pl.pallas_call(
        functools.partial(kernel, ny, nz, ntp),
        name="mixer_backward",
        out_shape=(
            tall,
            tall,
            tall,
            resident((1, channels), F32),
            resident((groups, taps), F32),
            resident((3, SHORT, channels), F32),
        ),
        in_specs=[pl.BlockSpec(memory_space=pltpu.HBM)] * 8,
        out_specs=(vmem,) * 6,
        scratch_shapes=[
            pltpu.VMEM((2, LANES), jnp.int32),
            pltpu.VMEM((channels,), BF16),
            pltpu.VMEM((groups, taps), BF16),
            pltpu.VMEM((3, SHORT, channels), BF16),
            pltpu.VMEM((3, rows, channels), BF16),
            pltpu.VMEM((rows, channels), BF16),
            pltpu.VMEM((3, nt, rows + 8, LANES), F32),
            pltpu.VMEM((3, nt, rows, LANES), F32),
            pltpu.VMEM((nt, rows, LANES), F32),
            pltpu.VMEM((nt, rows, LANES), F32),
            pltpu.VMEM((3, nt, rows + 8, LANES), F32),
            pltpu.VMEM((nt, rows + HALF, LANES), BF16),
            pltpu.VMEM((nt, rows + HALF, LANES), BF16),
            pltpu.VMEM((nt, 8 * HALF, LANES), BF16),
            pltpu.VMEM((nt, 8 * HALF, LANES), BF16),
            pltpu.VMEM((2, 2, HALF, LANES), BF16),
            pltpu.VMEM((2, 2, HALF, LANES), BF16),
            pltpu.VMEM((2, 2, HALF, LANES), F32),
            pltpu.VMEM((groups, LANES), F32),
            pltpu.VMEM((groups, LANES), F32),
            pltpu.VMEM((nt, 4, 8, LANES), F32),
            pltpu.VMEM((rows + 16, LANES), F32),
            pltpu.VMEM((rows + 8, LANES), F32),
            pltpu.VMEM((rows + 8, LANES), F32),
            pltpu.VMEM((2, LANES), jnp.int32),
            pltpu.VMEM((2, LANES), jnp.int32),
            pltpu.VMEM((8, channels), F32),
            pltpu.VMEM((8, channels), BF16),
            pltpu.VMEM((8, channels), BF16),
            pltpu.VMEM((8, channels), F32),
            pltpu.VMEM((8, channels), F32),
            pltpu.VMEM((8, channels), F32),
            pltpu.VMEM((8, channels), F32),
            pltpu.VMEM((2, 2, HALF, LANES), F32),
            pltpu.VMEM((ntp, 8, LANES), F32),
            pltpu.VMEM((2, 2, HALF, LANES), F32),
            pltpu.VMEM((2, 2, 8 * HALF, 2 * LANES), F32),
            pltpu.VMEM((2, 8 * HALF, LANES), F32),
            pltpu.VMEM((2, 2, 8 * HALF, LANES), BF16),
            pltpu.VMEM((nt, rows + HALF, LANES), BF16),
            pltpu.VMEM((nt, 16, LANES), F32),
            pltpu.VMEM((nt, 8, LANES), F32),
            pltpu.VMEM((ny, nt // ny, 16, LANES), F32),
            pltpu.VMEM((nz, nt // ny, 16, LANES), F32),
            pltpu.VMEM((nt, 16, LANES), F32),
            pltpu.VMEM((ny, nt // ny, 8, LANES), F32),
            pltpu.VMEM((nz, nt // ny, 8, LANES), F32),
            pltpu.VMEM((nt, 8, LANES), F32),
            dma((8,)),
            dma((4,)),
            dma((4,)),
            dma((nt,)),
            dma((nt,)),
            dma((nt,)),
            dma((nt,)),
            dma((ntp,)),
            dma((ntp,)),
            dma((2,)),
            dma((ny,)),
            dma((ny,)),
            dma((nz,)),
            dma((nz,)),
            dma((ny,)),
            dma((ny,)),
            dma((ny,)),
            dma((ny,)),
            dma((nz,)),
            dma((nz,)),
            dma((ny,)),
            dma((ny,)),
        ],
        compiler_params=pltpu.CompilerParams(
            collective_id=0, has_side_effects=True, vmem_limit_bytes=60 * 1024 * 1024
        ),
    )(
        q_in,
        k_in,
        v_in,
        grad_out,
        doc_ids.reshape(2, LANES),
        gain,
        filters,
        short_weight,
    )
    out = pl.pallas_call(
        publish,
        name="publish",
        out_shape=[jax.ShapeDtypeStruct(x.shape, x.dtype) for x in held],
        in_specs=[vmem] * 6,
        out_specs=[hbm] * 6,
        scratch_shapes=[dma((6,))],
    )(*[pinned(x) for x in held])
    return out[0], out[1], out[2], out[3].reshape(channels), out[4], out[5]


def solution(mesh, ring=RING):
    return jax.shard_map(
        functools.partial(on_device, ring),
        mesh=mesh,
        in_specs=(
            P("ctx", "tp"),
            P("ctx", "tp"),
            P("ctx", "tp"),
            P("ctx", "tp"),
            P("ctx"),
            P("tp"),
            P("tp", None),
            P(None, None, "tp"),
        ),
        out_specs=(
            P("ctx", "tp"),
            P("ctx", "tp"),
            P("ctx", "tp"),
            P("tp"),
            P("tp", None),
            P(None, None, "tp"),
        ),
        check_vma=False,
    )
```
